256 devices in a mesh: branch: 8 (over z), mp: 8 (over y_lo, x), dp: 4 (over y_hi, core).
Axes of the slice: x: 4, y: 4 (y_hi: 2, y_lo: 2; y = y_hi * 2 + y_lo), z: 8, core: 2. Of those that a mesh axis runs over, the one named last changes fastest.
Arguments:
- context: bfloat16 [4096, 4096], P(('branch', 'dp'), 'mp'), may hold values from -6 to 6
- residual: bfloat16 [4096, 4096], P(('branch', 'dp')), may hold values from -12 to 12
- attn_weight: bfloat16 [8, 4096, 4096], P('branch', 'mp', 'dp'), may hold values from -0.25 to 0.25
- norm_gain: bfloat16 [4096], replicated, may hold values from 0.099609375 to 1.8984375
- gate_weight: bfloat16 [8, 4096, 5504], P('branch', None, ('mp', 'dp')), may hold values from -0.09375 to 0.09375
- up_weight: bfloat16 [8, 4096, 5504], P('branch', None, ('mp', 'dp')), may hold values from -0.09375 to 0.09375
- down_weight: bfloat16 [8, 5504, 4096], P('branch', ('mp', 'dp')), may hold values from -0.078125 to 0.078125
- cotangent: bfloat16 [4096, 4096], P(('branch', 'dp')), may hold values from -0.796875 to 0.796875
- expert_ids: int32 [4096, 2], P(('branch', 'dp')), may hold values from 0 to 7, as said below
- gate_fixed: int32 [4096, 2], P(('branch', 'dp')), may hold values from 1 to 32767, as said below
Outputs:
- grad_gate: bfloat16 [8, 4096, 5504], P('branch', None, ('mp', 'dp'))
- grad_up: bfloat16 [8, 4096, 5504], P('branch', None, ('mp', 'dp'))
- grad_down: bfloat16 [8, 5504, 4096], P('branch', ('mp', 'dp'))
The draws below stay inside these ranges and needn't reach their ends.
Inputs may be any that keep to these rules, and one draw needn't show every extreme that they name: `expert_ids`: the two entries of a row differ; in every aligned block of 128 rows some expert is named by more than 40 choices. `gate_fixed`: the two entries of a row sum to 32768.
All inputs are finite; a program needn't handle non-finite values.
Results may differ from the reference program's by a relative error of at most 0.025.
Values may be sent and summed in bfloat16 or wider, within the bound.
A program may use at most 128 MiB of HBM per device.

```python
import math
import jax
import jax.numpy as jnp
from jax import lax

D = 4096
FF = 5504
TOK_DEV = 128
BRANCHES = 8
EXPERTS = 8
TOKENS = 4096
CAP = 40
N_MP = 8


def shuffle_group(group_key):
    return jax.random.permutation(group_key, TOK_DEV)


def route_table(key):
    base_key = jax.random.fold_in(key, 17)
    key_hot, key_perm, key_first, key_second = jax.random.split(base_key, 4)
    groups = TOKENS // TOK_DEV
    hot_expert = jax.random.randint(key_hot, (), 0, EXPERTS)
    ranking = jax.vmap(shuffle_group)(jax.random.split(key_perm, groups))
    hot_count = min(TOK_DEV, CAP + CAP // 4)
    chosen = ranking < hot_count
    other_pick = (hot_expert + 1 + jax.random.randint(key_first, (groups, TOK_DEV), 0, EXPERTS - 1)) % EXPERTS
    first_pick = jnp.where(chosen, hot_expert, other_pick)
    second = (first_pick + 1 + jax.random.randint(key_second, (groups, TOK_DEV), 0, EXPERTS - 1)) % EXPERTS
    expert_table = jnp.stack([first_pick, second], axis=2).reshape(TOKENS, 2)
    return expert_table.astype(jnp.int32)


def draw_expert_ids(key, part):
    return route_table(key)


def draw_gate_fixed(key, part):
    first_part = jax.random.randint(jax.random.fold_in(key, 31), (TOKENS, 1), 1, 32768)
    return jnp.concatenate([first_part, 32768 - first_part], axis=1).astype(jnp.int32)


def draw_residual(key, part):
    key_base, key_rows, key_cols = jax.random.split(jax.random.fold_in(key, 23), 3)
    values = jax.random.normal(key_base, (TOKENS, D), jnp.float32)
    row_scale = jnp.exp(jax.random.uniform(key_rows, (TOKENS, 1), jnp.float32, math.log(0.3), math.log(3.0)))
    col_scale = jnp.exp(jax.random.uniform(key_cols, (1, D), jnp.float32, math.log(0.5), math.log(2.0)))
    values = values * row_scale * col_scale
    return jnp.clip(values, -12.0, 12.0).astype(jnp.bfloat16)


def levels(own_key, shape, cuts, least, largest):
    loudness = 1.0
    for dim, blocks in cuts:
        draws = jax.random.uniform(jax.random.fold_in(jax.random.fold_in(own_key, 6), dim), (blocks,), jnp.float32, least / len(cuts), largest / len(cuts))
        loudness = loudness * jnp.repeat(jnp.exp(draws), shape[dim] // blocks).reshape((-1,) + (1,) * (len(shape) - 1 - dim))
    return loudness


def noise(own_key, shape, width, most, shards=(), held_as=jnp.bfloat16):
    result = jax.random.normal(own_key, shape, jnp.float32) * width
    if len(shards) > 0:
        result = levels(own_key, shape, shards, -0.22, 0.18) * result
    return jnp.clip(result, min=-most, max=most).astype(held_as)


def setup_inputs(seed: int = 0) -> dict:
    key_of = jax.random.split(jax.random.key(seed), 11)
    context = noise(key_of[0], (TOKENS, D), 1.0, 6.0, ((0, 32), (1, 8)))
    residual = draw_residual(jax.random.fold_in(key_of[10], 71), 0)
    attn_weight = noise(key_of[2], (BRANCHES, D, D), (D // BRANCHES) ** -0.5, 0.25, ((0, 8), (1, 8), (2, 4)))
    norm_gain = jnp.clip(1.0 + 0.18 * jax.random.normal(key_of[3], (D,), jnp.float32), 0.099609375, 1.8984375).astype(jnp.bfloat16)
    gate_weight = noise(key_of[4], (EXPERTS, D, FF), D ** -0.5, 0.09375, ((0, 8), (2, 32)))
    up_weight = noise(key_of[5], (EXPERTS, D, FF), D ** -0.5, 0.09375, ((0, 8), (2, 32)))
    down_weight = noise(key_of[6], (EXPERTS, FF, D), FF ** -0.5, 0.078125, ((0, 8), (1, 32)))
    cotangent = noise(key_of[7], (TOKENS, D), 0.1, 0.796875, ((0, 32),))
    expert_ids = draw_expert_ids(jax.random.fold_in(key_of[10], 71), 0)
    gate_fixed = draw_gate_fixed(jax.random.fold_in(key_of[10], 71), 0)
    return {"context": context, "residual": residual, "attn_weight": attn_weight, "norm_gain": norm_gain, "gate_weight": gate_weight, "up_weight": up_weight, "down_weight": down_weight, "cotangent": cotangent, "expert_ids": expert_ids, "gate_fixed": gate_fixed}


def slot_positions(id_block, capacity, experts):
    rows = id_block.shape[0]
    picks = jnp.concatenate([id_block[:, 0], id_block[:, 1]], axis=0)
    onehot = (picks[:, None] == jnp.arange(experts, dtype=jnp.int32)[None, :]).astype(jnp.int32)
    position = lax.optimization_barrier(jnp.sum((jnp.cumsum(onehot, axis=0) - 1) * onehot, axis=1))
    position = jnp.where(position < capacity, position, -1)
    return jnp.stack([position[:rows], position[rows:]], axis=1).astype(jnp.int32)

def expert_grads(operands):
    expert_in, expert_cot, w_gate, w_up, w_down = operands
    pre_gate = jnp.dot(expert_in, w_gate, preferred_element_type=jnp.float32)
    pre_up = jnp.dot(expert_in, w_up, preferred_element_type=jnp.float32)
    sigmoid_gate = jax.nn.sigmoid(pre_gate)
    active = pre_gate * sigmoid_gate
    hidden = (active * pre_up).astype(jnp.bfloat16)
    grad_down = jnp.dot(hidden.T, expert_cot, preferred_element_type=jnp.float32)
    back_grad = jnp.dot(expert_cot, w_down.T, preferred_element_type=jnp.float32)
    d_gate = (back_grad * pre_up * sigmoid_gate * (1.0 + pre_gate * (1.0 - sigmoid_gate))).astype(jnp.bfloat16)
    d_up = (back_grad * active).astype(jnp.bfloat16)
    grad_gate = jnp.dot(expert_in.T, d_gate, preferred_element_type=jnp.float32)
    grad_up = jnp.dot(expert_in.T, d_up, preferred_element_type=jnp.float32)
    return (grad_gate.astype(jnp.bfloat16), grad_up.astype(jnp.bfloat16), grad_down.astype(jnp.bfloat16))

def reference(context, residual, attn_weight, norm_gain, gate_weight, up_weight, down_weight, cotangent, expert_ids, gate_fixed):
    summed = lax.optimization_barrier(jnp.sum(attn_weight.astype(jnp.float32), axis=0))
    merged = (summed / BRANCHES).astype(jnp.bfloat16)
    feature_block = D // N_MP
    attention = jnp.zeros((TOKENS, D), jnp.float32)
    for block_index in range(N_MP):
        low = block_index * feature_block
        partial_value = jnp.dot(context[:, low:low + feature_block], merged[low:low + feature_block, :], preferred_element_type=jnp.float32)
        partial_value = lax.optimization_barrier(partial_value.astype(jnp.bfloat16))
        attention = attention + partial_value.astype(jnp.float32)
    mixed_in = residual.astype(jnp.float32) + attention
    inv_rms = lax.rsqrt(lax.optimization_barrier(jnp.mean(mixed_in * mixed_in, axis=1, keepdims=True)) + 1e-05)
    normed = (mixed_in * inv_rms * norm_gain.astype(jnp.float32)[None, :]).astype(jnp.bfloat16)
    groups = TOKENS // TOK_DEV
    slots = jax.vmap(lambda blk: slot_positions(blk, CAP, EXPERTS))(expert_ids.reshape(groups, TOK_DEV, 2)).reshape(TOKENS, 2)
    token_index = jnp.arange(TOKENS, dtype=jnp.int32)
    group_index = token_index // TOK_DEV
    is_valid = slots >= 0
    destination = (expert_ids * groups + group_index[:, None]) * CAP + slots
    destination = jnp.where(is_valid, destination, EXPERTS * groups * CAP).astype(jnp.int32)
    slot_token = jnp.full((EXPERTS * groups * CAP,), -1, jnp.int32)
    slot_token = slot_token.at[destination.reshape(-1)].set(jnp.broadcast_to(token_index[:, None], (TOKENS, 2)).reshape(-1), mode='drop')
    slot_gate = jnp.zeros((EXPERTS * groups * CAP,), jnp.float32)
    slot_gate = slot_gate.at[destination.reshape(-1)].set((gate_fixed.astype(jnp.float32) / 32768.0).reshape(-1), mode='drop')
    present = slot_token >= 0
    safe_index = jnp.maximum(slot_token, 0).astype(jnp.int32)
    rows_in = jnp.where(present[:, None], normed[safe_index], jnp.zeros((), jnp.bfloat16))
    rows_cot = (slot_gate[:, None] * cotangent[safe_index].astype(jnp.float32)).astype(jnp.bfloat16)
    rows_in = rows_in.reshape(EXPERTS, groups * CAP, D)
    rows_cot = rows_cot.reshape(EXPERTS, groups * CAP, D)
    results = lax.map(expert_grads, (rows_in, rows_cot, gate_weight, up_weight, down_weight))
    return (results[0], results[1], results[2])
```

```python
import functools

import jax
import jax.numpy as jnp
from jax import lax
from jax.experimental import pallas as pl
from jax.experimental.pallas import tpu as pltpu
from jax.sharding import PartitionSpec as P

MESH = pl.DeviceIdType.MESH
BF = jnp.bfloat16
F32 = jnp.float32
NT = (((1,), (1,)), ((), ()))


def slot_positions(id_block, capacity, experts):
    rows = id_block.shape[0]
    picks = jnp.concatenate([id_block[:, 0], id_block[:, 1]], axis=0)
    onehot = (picks[:, None] == jnp.arange(experts, dtype=jnp.int32)[None, :]).astype(jnp.int32)
    position = jnp.sum((jnp.cumsum(onehot, axis=0) - 1) * onehot, axis=1)
    position = jnp.where(position < capacity, position, -1)
    return jnp.stack([position[:rows], position[rows:]], axis=1)


class Coords:
    def __init__(self):
        self.z = lax.axis_index("branch")
        self.mp = lax.axis_index("mp")
        self.dp = lax.axis_index("dp")
        self.x = lax.rem(self.mp, 4)
        self.core = lax.rem(self.dp, 2)
        self.y = lax.div(self.dp, 2) * 2 + lax.div(self.mp, 4)

    def at(self, da, db, core):
        other = 1 - core
        x = lax.rem(self.x + other * da + core * db + 8, 4)
        y = lax.rem(self.y + core * da + other * db + 8, 4)
        return x, y

    def device(self, da, db):
        x, y = self.at(da, db, self.core)
        return (self.z, lax.rem(y, 2) * 4 + x, lax.div(y, 2) * 2 + self.core)

    def piece(self, da, db, core=None):
        core = self.core if core is None else core
        x, y = self.at(da, db, core)
        return (lax.div(y, 2) * 2 + core) * 8 + lax.rem(y, 2) * 4 + x

    def sibling(self):
        return (self.z, self.mp, self.dp + 1 - 2 * self.core)


RING = (0, -1, 1, 2)


class PlaneGather:
    COPIES = 36

    def __init__(self, at, buf, send, recv):
        self.at, self.buf, self.send, self.recv = at, buf, send, recv
        self.half = buf.shape[1] // 2
        self.sent = []

    def view(self, piece, half=None):
        if half is None:
            return self.buf.at[piece]
        return self.buf.at[piece, pl.ds(half * self.half, self.half)]

    def copy(self, index, piece, device, half=None):
        ref = self.view(piece, half)
        return pltpu.make_async_remote_copy(
            src_ref=ref,
            dst_ref=ref,
            send_sem=self.send.at[index],
            recv_sem=self.recv.at[index],
            device_id=device,
            device_id_type=MESH,
        )

    def go(self, index, piece, device, half=None):
        descriptor = self.copy(index, piece, device, half)
        descriptor.start()
        self.sent.append(descriptor)

    def arrived(self, index, piece, half=None):
        self.copy(index, piece, self.at.sibling(), half).wait_recv()

    def to_sibling(self, qa, qb):
        index = 20 + 4 * RING.index(qa) + RING.index(qb)
        self.go(index, self.at.piece(qa, qb), self.at.sibling())

    def spread(self, qa):
        index = 4 + 4 * RING.index(qa)
        piece = self.at.piece(qa, 0)
        self.go(index, piece, self.at.device(0, 1))
        self.go(index + 1, piece, self.at.device(0, -1))
        self.to_sibling(qa, 0)

    def start(self):
        piece = self.at.piece(0, 0)
        self.go(0, piece, self.at.device(1, 0))
        self.go(1, piece, self.at.device(-1, 0))
        self.spread(0)

    def first_axis(self):
        low, high = self.at.piece(-1, 0), self.at.piece(1, 0)
        self.arrived(0, low)
        self.go(2, low, self.at.device(1, 0), 0)
        self.arrived(1, high)
        self.go(3, high, self.at.device(-1, 0), 1)
        self.spread(-1)
        self.spread(1)

    def first_axis_far(self):
        far = self.at.piece(2, 0)
        self.arrived(2, far, 0)
        self.arrived(3, far, 1)
        self.spread(2)

    def relay(self, qa):
        index = 4 + 4 * RING.index(qa)
        low, high = self.at.piece(qa, -1), self.at.piece(qa, 1)
        self.arrived(index, low)
        self.go(index + 2, low, self.at.device(0, 1), 0)
        self.arrived(index + 1, high)
        self.go(index + 3, high, self.at.device(0, -1), 1)
        self.to_sibling(qa, -1)
        self.to_sibling(qa, 1)

    def far(self, qa):
        index = 4 + 4 * RING.index(qa)
        piece = self.at.piece(qa, 2)
        self.arrived(index + 2, piece, 0)
        self.arrived(index + 3, piece, 1)
        self.to_sibling(qa, 2)

    def from_sibling(self, qa):
        for qb in RING:
            index = 20 + 4 * RING.index(qa) + RING.index(qb)
            self.arrived(index, self.at.piece(qa, qb, 1 - self.at.core))

    def own_group(self, qa):
        return [self.at.piece(qa, qb) for qb in RING]

    def sibling_group(self, qa):
        return [self.at.piece(qa, qb, 1 - self.at.core) for qb in RING]

    def steps(self):
        return [
            self.start,
            self.first_axis,
            functools.partial(self.relay, 0),
            self.first_axis_far,
            functools.partial(self.relay, -1),
            functools.partial(self.relay, 1),
            functools.partial(self.far, 0),
            functools.partial(self.relay, 2),
            functools.partial(self.far, -1),
            functools.partial(self.far, 1),
            functools.partial(self.far, 2),
        ]

    def finish(self):
        for descriptor in self.sent:
            descriptor.wait_send()


def kernel(
    attn_ref, context_ref, residual_ref, cot_ref, info_ref, gain_ref, wg_ref, wu_ref, wd_ref,
    og_ref, ou_ref, od_ref,
    rows_in, rows_cot, ctx_all, wgu, wd, wtmp, acc, acc_back, ssq, dgu, hid,
    red_in_p, red_in_m, red_out_p, red_out_m, red_sum, merged_all,
    res_all, cot_all, info_all, sel, route_x, route_c,
    w_sem, in_send, in_recv, in_local, cot_send, cot_recv, ctx_send, ctx_recv,
    ex_send, ex_recv, ex_local, rp_send, rp_recv, rm_send, rm_recv,
    ma_send, ma_recv, ga_send, ga_recv, tx_send, tx_recv, tc_send, tc_recv,
):
    at = Coords()
    z, mp, dp = at.z, at.mp, at.dp
    own = at.piece(0, 0)
    hidden = wg_ref.shape[0]
    hid_pad = wgu.shape[0] // 2
    pending = []

    def z_dev(k):
        return (lax.rem(z + k + 8, 8), mp, dp)

    def mp_dev(k):
        return (z, lax.rem(mp + k, 8), dp)

    def dp_dev(k):
        return (z, mp, lax.rem(dp + k, 4))

    def remote(src, dst, send, recv, device):
        return pltpu.make_async_remote_copy(
            src_ref=src, dst_ref=dst, send_sem=send, recv_sem=recv,
            device_id=device, device_id_type=MESH,
        )

    def push(src, dst, send, recv, device):
        descriptor = remote(src, dst, send, recv, device)
        descriptor.start()
        pending.append(descriptor)

    def landed(dst, recv, send):
        remote(dst, dst, send, recv, at.sibling()).wait_recv()

    barrier = pltpu.get_barrier_semaphore()
    peers = [z_dev(k) for k in range(1, 8)] + [mp_dev(k) for k in range(1, 8)]
    peers += [dp_dev(k) for k in range(1, 4)]
    for dy in (1, -1):
        y = lax.rem(at.y + dy + 4, 4)
        peers.append((z, lax.rem(y, 2) * 4 + at.x, lax.div(y, 2) * 2 + at.core))
    for peer in peers:
        pl.semaphore_signal(barrier, inc=1, device_id=peer, device_id_type=MESH)

    weights = [
        pltpu.make_async_copy(wg_ref, wtmp.at[0], w_sem.at[0]),
        pltpu.make_async_copy(wu_ref, wtmp.at[1], w_sem.at[1]),
        pltpu.make_async_copy(wd_ref, wd, w_sem.at[2]),
    ]
    ctx_copy = pltpu.make_async_copy(context_ref, ctx_all.at[own], in_local.at[0])
    ctx_copy.start()
    dp_rows = pl.ds(pl.multiple_of(dp * 128, 128), 128)

    def columns(k):
        d = lax.rem(dp + k, 4)
        return pl.ds(pl.multiple_of(d * 1024 + mp * 128, 128), 128)

    locals_ = [
        pltpu.make_async_copy(residual_ref.at[:, columns(0)], res_all.at[dp_rows], ex_local.at[0]),
        pltpu.make_async_copy(cot_ref.at[:, columns(0)], cot_all.at[dp_rows], ex_local.at[1]),
        pltpu.make_async_copy(info_ref, info_all.at[dp], ex_local.at[2]),
    ]
    for copy in locals_:
        copy.start()
    for copy in weights:
        copy.start()
    pl.semaphore_wait(barrier, len(peers))

    for k in range(1, 4):
        push(cot_ref.at[:, columns(k)], cot_all.at[dp_rows], ex_send.at[0, k], ex_recv.at[0, k], dp_dev(k))
        push(info_ref, info_all.at[dp], ex_send.at[1, k], ex_recv.at[1, k], dp_dev(k))

    def chunk(k):
        t = lax.rem(z + k + 8, 8)
        return pl.ds(pl.multiple_of(t * 64, 64), 64)

    half_cols = [pl.ds(0, 512), pl.ds(512, 512)]

    def reduce_step(step):
        for h in range(2):
            cols = half_cols[h]
            if step < 4:
                src = attn_ref.at[chunk(4), cols]
                if step > 0:
                    landed(red_in_p.at[step - 1, h], rp_recv.at[step - 1, h], rp_send.at[step - 1, h])
                    red_out_p[step - 1, h] = (
                        red_in_p[step - 1, h].astype(F32) + attn_ref[chunk(4 - step), cols].astype(F32)
                    ).astype(BF)
                    src = red_out_p.at[step - 1, h]
                push(src, red_in_p.at[step, h], rp_send.at[step, h], rp_recv.at[step, h], z_dev(1))
            if step < 3:
                src = attn_ref.at[chunk(-3), cols]
                if step > 0:
                    landed(red_in_m.at[step - 1, h], rm_recv.at[step - 1, h], rm_send.at[step - 1, h])
                    red_out_m[step - 1, h] = (
                        red_in_m[step - 1, h].astype(F32) + attn_ref[chunk(step - 3), cols].astype(F32)
                    ).astype(BF)
                    src = red_out_m.at[step - 1, h]
                push(src, red_in_m.at[step, h], rm_send.at[step, h], rm_recv.at[step, h], z_dev(-1))

    reduce_step(0)
    for k in range(1, 4):
        push(residual_ref.at[:, columns(k)], res_all.at[dp_rows], ex_send.at[2, k], ex_recv.at[2, k], dp_dev(k))

    ctx_gather = PlaneGather(at, ctx_all, ctx_send, ctx_recv)
    cot_gather = PlaneGather(at, rows_cot, cot_send, cot_recv)
    in_gather = PlaneGather(at, rows_in, in_send, in_recv)
    ctx_copy.wait()
    ctx_steps = ctx_gather.steps()
    cot_steps = cot_gather.steps()
    in_steps = in_gather.steps()
    ctx_steps.pop(0)()

    def from_group(k):
        d = lax.rem(dp - k + 4, 4)
        return pl.ds(pl.multiple_of(d * 128, 128), 128), d

    locals_[1].wait()
    locals_[2].wait()
    for k in range(1, 4):
        rows, d = from_group(k)
        landed(cot_all.at[rows], ex_recv.at[0, k], ex_send.at[0, k])
        landed(info_all.at[d], ex_recv.at[1, k], ex_send.at[1, k])

    @pl.loop(0, 8)
    def _(e):
        place = (lax.broadcasted_iota(jnp.int32, (160, 128), 0) + e * 160).astype(F32)
        row_gate = jnp.zeros((160, 1), F32)
        rows = pl.ds(pl.multiple_of(e * 160, 160), 160)
        for d in range(4):
            info = info_all[d]
            first = place == info[0:1, :]
            second = place == info[1:2, :]
            sel[rows, d * 128:(d + 1) * 128] = jnp.where(first | second, 1.0, 0.0).astype(BF)
            gates = jnp.where(first, info[2:3, :], jnp.where(second, info[3:4, :], 0.0))
            row_gate += jnp.sum(gates, axis=1, keepdims=True)
        picked = jnp.dot(sel[rows, :], cot_all[...], preferred_element_type=F32)
        route_c[e] = (picked * row_gate).astype(BF)

    own_block = pl.ds(pl.multiple_of(z * 160, 160), 160)

    def exchange(route, gathered, send, recv):
        for k in range(1, 8):
            e = lax.rem(z + k, 8)
            push(route.at[e], gathered.at[own, own_block], send.at[k], recv.at[k], z_dev(k))
        gathered[own, own_block, :] = route[z]

    def exchanged(gathered, send, recv):
        for k in range(1, 8):
            b = lax.rem(z - k + 8, 8)
            landed(gathered.at[own, pl.ds(pl.multiple_of(b * 160, 160), 160)], recv.at[k], send.at[k])

    exchange(route_c, rows_cot, tc_send, tc_recv)

    reduce_step(1)
    ctx_steps.pop(0)()
    reduce_step(2)
    ctx_steps.pop(0)()
    ctx_steps.pop(0)()
    reduce_step(3)
    ctx_steps.pop(0)()
    ctx_steps.pop(0)()

    for h in range(2):
        landed(red_in_p.at[3, h], rp_recv.at[3, h], rp_send.at[3, h])
        landed(red_in_m.at[2, h], rm_recv.at[2, h], rm_send.at[2, h])
        total = (
            red_in_p[3, h].astype(F32) + red_in_m[2, h].astype(F32)
            + attn_ref[chunk(0), half_cols[h]].astype(F32)
        )
        mean = (total * 0.125).astype(BF)
        for part in range(4):
            red_sum[4 * h + part] = mean[:, part * 128:(part + 1) * 128]
    own_rows = pl.ds(pl.multiple_of(z * 64, 64), 64)
    for k in range(1, 8):
        j = lax.rem(mp + k, 8)
        push(red_sum.at[j], merged_all.at[mp, own_rows], ma_send.at[k], ma_recv.at[k], mp_dev(k))
    merged_all[mp, own_rows, :] = red_sum[mp]
    ctx_steps.pop(0)()
    exchanged(rows_cot, tc_send, tc_recv)
    cot_steps.pop(0)()
    for k in range(1, 8):
        j = lax.rem(mp - k + 8, 8)
        landed(merged_all.at[j, own_rows], ma_recv.at[k], ma_send.at[k])

    def merged_view(k, h):
        t = lax.rem(z + k + 8, 8)
        return merged_all.at[pl.ds(4 * h, 4), pl.ds(pl.multiple_of(t * 64, 64), 64)]

    def gather_step(step):
        for h in range(2):
            if step < 5 and step > 0:
                landed(merged_view(-step, h), ga_recv.at[0, step - 1, h], ga_send.at[0, step - 1, h])
            if step < 4:
                view = merged_view(-step, h)
                push(view, view, ga_send.at[0, step, h], ga_recv.at[0, step, h], z_dev(1))
            if step < 4 and step > 0:
                landed(merged_view(step, h), ga_recv.at[1, step - 1, h], ga_send.at[1, step - 1, h])
            if step < 3:
                view = merged_view(step, h)
                push(view, view, ga_send.at[1, step, h], ga_recv.at[1, step, h], z_dev(-1))

    gather_step(0)
    for copy in weights:
        copy.wait()
    wgu[0:hidden, :] = wtmp[0]
    wgu[hid_pad:hid_pad + hidden, :] = wtmp[1]
    acc[...] = jnp.zeros_like(acc)
    acc_back[...] = jnp.zeros_like(acc_back)
    ssq[...] = jnp.zeros_like(ssq)
    while ctx_steps:
        ctx_steps.pop(0)()
    gather_step(1)
    cot_steps.pop(0)()
    gather_step(2)
    cot_steps.pop(0)()
    gather_step(3)
    cot_steps.pop(0)()
    for qa in RING:
        ctx_gather.from_sibling(qa)
    gather_step(4)
    for k in range(1, 4):
        rows, _ = from_group(k)
        landed(res_all.at[rows], ex_recv.at[2, k], ex_send.at[2, k])
    locals_[0].wait()

    own_gain = gain_ref[pl.ds(own, 1), :]

    for d in range(4):
        total = jnp.zeros((128, 128), F32)
        for j in range(8):
            total += jnp.dot(ctx_all[d * 8 + j], merged_all[j], preferred_element_type=F32)
        rows = slice(d * 128, (d + 1) * 128)
        mixed = total + res_all[rows, :].astype(F32)
        res_all[rows, :] = (mixed * own_gain).astype(BF)

    @pl.loop(0, 8)
    def _(e):
        rows = pl.ds(pl.multiple_of(e * 160, 160), 160)
        route_x[e] = jnp.dot(sel[rows, :], res_all[...], preferred_element_type=F32).astype(BF)

    exchange(route_x, rows_in, tx_send, tx_recv)
    cot_steps.pop(0)()
    cot_steps.pop(0)()
    exchanged(rows_in, tx_send, tx_recv)
    in_steps.pop(0)()
    while cot_steps:
        cot_steps.pop(0)()

    blocks = 5
    width = acc.shape[1] // blocks

    def lanes(piece):
        return pl.ds(pl.multiple_of(piece * 128, 128), 128)

    def back_group(group):
        lhs = jnp.concatenate([wd[:, lanes(p)] for p in group], axis=1)

        @pl.loop(0, blocks)
        def _(n):
            rows = pl.ds(pl.multiple_of(n * width, width), width)
            rhs = jnp.concatenate([rows_cot[p, rows, :] for p in group], axis=1)
            acc_back[:, rows] += lax.dot_general(lhs, rhs, NT, preferred_element_type=F32)

    def fore_group(group):
        lhs = jnp.concatenate([wgu[:, lanes(p)] for p in group], axis=1)
        inverse = jnp.concatenate([1.0 / gain_ref[pl.ds(p, 1), :] for p in group], axis=1)
        ones = jnp.ones((8, 512), BF)

        @pl.loop(0, blocks)
        def _(n):
            rows = pl.ds(pl.multiple_of(n * width, width), width)
            rhs = jnp.concatenate([rows_in[p, rows, :] for p in group], axis=1)
            acc[:, rows] += lax.dot_general(lhs, rhs, NT, preferred_element_type=F32)
            scaled = rhs.astype(F32) * inverse
            ssq[:, rows] += lax.dot_general(
                ones, (scaled * scaled).astype(BF), NT, preferred_element_type=F32
            )

    back_group(cot_gather.own_group(0))
    back_group(cot_gather.own_group(-1))
    in_steps.pop(0)()
    back_group(cot_gather.own_group(1))
    back_group(cot_gather.own_group(2))
    in_steps.pop(0)()
    for qa in RING[:2]:
        cot_gather.from_sibling(qa)
        back_group(cot_gather.sibling_group(qa))
    in_steps.pop(0)()
    for qa in RING[2:]:
        cot_gather.from_sibling(qa)
        back_group(cot_gather.sibling_group(qa))
    while in_steps:
        in_steps.pop(0)()
    for qa in RING:
        fore_group(in_gather.own_group(qa))
    for qa in RING:
        in_gather.from_sibling(qa)
        fore_group(in_gather.sibling_group(qa))

    @pl.loop(0, blocks)
    def _(n):
        rows = pl.ds(pl.multiple_of(n * width, width), width)
        inv = lax.rsqrt(ssq[0:1, rows] * (1.0 / 4096.0) + 1e-05)
        gate = acc[0:hidden, rows] * inv
        up = acc[hid_pad:hid_pad + hidden, rows] * inv
        back = acc_back[:, rows]
        sig = jax.nn.sigmoid(gate)
        active = gate * sig
        hid[:, rows] = (active * up).astype(BF)
        back = back * inv
        dgu[0:hidden, rows] = (back * up * sig * (1.0 + gate * (1.0 - sig))).astype(BF)
        dgu[hid_pad:hid_pad + hidden, rows] = (back * active).astype(BF)

    @pl.loop(0, 16)
    def _(n):
        cols = pl.ds(pl.multiple_of(n * 256, 256), 256)
        rhs = jnp.concatenate([rows_in[2 * n], rows_in[2 * n + 1]], axis=1)
        both = jnp.dot(dgu[...], rhs, preferred_element_type=F32).astype(BF)
        og_ref[:, cols] = both[0:hidden]
        ou_ref[:, cols] = both[hid_pad:hid_pad + hidden]
        rhs = jnp.concatenate([rows_cot[2 * n], rows_cot[2 * n + 1]], axis=1)
        od_ref[:, cols] = jnp.dot(hid[...], rhs, preferred_element_type=F32).astype(BF)

    for gather in (ctx_gather, cot_gather, in_gather):
        gather.finish()
    for descriptor in pending:
        descriptor.wait_send()


def per_device(
    context, residual, attn_weight, norm_gain, gate_weight, up_weight, down_weight,
    cotangent, expert_ids, gate_fixed,
):
    slots = slot_positions(expert_ids, 40, 8)
    code = jnp.where(slots >= 0, expert_ids * 160 + lax.axis_index("dp") * 40 + slots, -1)
    info = jnp.concatenate(
        [
            code.T.astype(jnp.float32),
            gate_fixed.T.astype(jnp.float32) / 32768.0,
            jnp.zeros((4, 128), jnp.float32),
        ],
        axis=0,
    )
    gain = norm_gain.astype(jnp.float32).reshape(32, 128)
    hidden = gate_weight.shape[2]
    pad = 176
    dma = pltpu.SemaphoreType.DMA
    vmem = pl.BlockSpec(memory_space=pltpu.VMEM)
    hbm = pl.BlockSpec(memory_space=pl.ANY)
    out = jax.ShapeDtypeStruct((hidden, 4096), BF)
    copies = PlaneGather.COPIES
    grads = pl.pallas_call(
        kernel,
        out_shape=(out, out, out),
        in_specs=[vmem, hbm, hbm, hbm, hbm, vmem, hbm, hbm, hbm],
        out_specs=(vmem, vmem, vmem),
        scratch_shapes=[
            pltpu.VMEM((32, 1280, 128), BF),
            pltpu.VMEM((32, 1280, 128), BF),
            pltpu.VMEM((32, 128, 512), BF),
            pltpu.VMEM((2 * pad, 4096), BF),
            pltpu.VMEM((hidden, 4096), BF),
            pltpu.VMEM((2, hidden, 4096), BF),
            pltpu.VMEM((2 * pad, 1280), F32),
            pltpu.VMEM((hidden, 1280), F32),
            pltpu.VMEM((8, 1280), F32),
            pltpu.VMEM((2 * pad, 1280), BF),
            pltpu.VMEM((hidden, 1280), BF),
            pltpu.VMEM((4, 2, 64, 512), BF),
            pltpu.VMEM((3, 2, 64, 512), BF),
            pltpu.VMEM((3, 2, 64, 512), BF),
            pltpu.VMEM((2, 2, 64, 512), BF),
            pltpu.VMEM((8, 64, 128), BF),
            pltpu.VMEM((8, 512, 128), BF),
            pltpu.VMEM((512, 128), BF),
            pltpu.VMEM((512, 128), BF),
            pltpu.VMEM((4, 8, 128), F32),
            pltpu.VMEM((1280, 512), BF),
            pltpu.VMEM((8, 160, 128), BF),
            pltpu.VMEM((8, 160, 128), BF),
            dma((3,)),
            dma((copies,)), dma((copies,)), dma((1,)),
            dma((copies,)), dma((copies,)),
            dma((copies,)), dma((copies,)),
            dma((3, 4)), dma((3, 4)), dma((3,)),
            dma((4, 2)), dma((4, 2)), dma((3, 2)), dma((3, 2)),
            dma((8,)), dma((8,)),
            dma((2, 4, 2)), dma((2, 4, 2)),
            dma((8,)), dma((8,)),
            dma((8,)), dma((8,)),
        ],
        compiler_params=pltpu.CompilerParams(
            collective_id=0, has_side_effects=True, vmem_limit_bytes=66 * 1000 * 1000
        ),
    )(
        attn_weight[0], context, residual, cotangent, info, gain,
        gate_weight[0].T, up_weight[0].T, down_weight[0],
    )
    return grads[0].T[None], grads[1].T[None], grads[2][None]


def solution(mesh):
    return jax.shard_map(
        per_device,
        mesh=mesh,
        in_specs=(
            P(("branch", "dp"), "mp"),
            P(("branch", "dp"), None),
            P("branch", "mp", "dp"),
            P(),
            P("branch", None, ("mp", "dp")),
            P("branch", None, ("mp", "dp")),
            P("branch", ("mp", "dp"), None),
            P(("branch", "dp"), None),
            P(("branch", "dp"), None),
            P(("branch", "dp"), None),
        ),
        out_specs=(
            P("branch", None, ("mp", "dp")),
            P("branch", None, ("mp", "dp")),
            P("branch", ("mp", "dp"), None),
        ),
        check_vma=False,
    )
```

```python
import functools

import jax
import jax.numpy as jnp
from jax import lax
from jax.experimental import pallas as pl
from jax.experimental.pallas import tpu as pltpu
from jax.sharding import PartitionSpec as P

MESH = pl.DeviceIdType.MESH
BF = jnp.bfloat16
F32 = jnp.float32
NT = (((1,), (1,)), ((), ()))


class Coords:
    def __init__(self):
        self.z = lax.axis_index("branch")
        self.mp = lax.axis_index("mp")
        self.dp = lax.axis_index("dp")
        self.x = lax.rem(self.mp, 4)
        self.core = lax.rem(self.dp, 2)
        self.y = lax.div(self.dp, 2) * 2 + lax.div(self.mp, 4)

    def at(self, da, db, core):
        other = 1 - core
        x = lax.rem(self.x + other * da + core * db + 8, 4)
        y = lax.rem(self.y + core * da + other * db + 8, 4)
        return x, y

    def device(self, da, db):
        x, y = self.at(da, db, self.core)
        return (self.z, lax.rem(y, 2) * 4 + x, lax.div(y, 2) * 2 + self.core)

    def piece(self, da, db, core=None):
        core = self.core if core is None else core
        x, y = self.at(da, db, core)
        return (lax.div(y, 2) * 2 + core) * 8 + lax.rem(y, 2) * 4 + x

    def sibling(self):
        return (self.z, self.mp, self.dp + 1 - 2 * self.core)


RING = (0, -1, 1, 2)


class PlaneGather:
    COPIES = 36

    def __init__(self, at, buf, send, recv):
        self.at, self.buf, self.send, self.recv = at, buf, send, recv
        self.half = buf.shape[1] // 2
        self.sent = []

    def view(self, piece, half=None):
        if half is None:
            return self.buf.at[piece]
        return self.buf.at[piece, pl.ds(half * self.half, self.half)]

    def copy(self, index, piece, device, half=None):
        ref = self.view(piece, half)
        return pltpu.make_async_remote_copy(
            src_ref=ref,
            dst_ref=ref,
            send_sem=self.send.at[index],
            recv_sem=self.recv.at[index],
            device_id=device,
            device_id_type=MESH,
        )

    def go(self, index, piece, device, half=None):
        descriptor = self.copy(index, piece, device, half)
        descriptor.start()
        self.sent.append(descriptor)

    def arrived(self, index, piece, half=None):
        self.copy(index, piece, self.at.sibling(), half).wait_recv()

    def to_sibling(self, qa, qb):
        index = 20 + 4 * RING.index(qa) + RING.index(qb)
        self.go(index, self.at.piece(qa, qb), self.at.sibling())

    def spread(self, qa):
        index = 4 + 4 * RING.index(qa)
        piece = self.at.piece(qa, 0)
        self.go(index, piece, self.at.device(0, 1))
        self.go(index + 1, piece, self.at.device(0, -1))
        self.to_sibling(qa, 0)

    def start(self):
        piece = self.at.piece(0, 0)
        self.go(0, piece, self.at.device(1, 0))
        self.go(1, piece, self.at.device(-1, 0))
        self.spread(0)

    def first_axis(self):
        low, high = self.at.piece(-1, 0), self.at.piece(1, 0)
        self.arrived(0, low)
        self.go(2, low, self.at.device(1, 0), 0)
        self.arrived(1, high)
        self.go(3, high, self.at.device(-1, 0), 1)
        self.spread(-1)
        self.spread(1)

    def first_axis_far(self):
        far = self.at.piece(2, 0)
        self.arrived(2, far, 0)
        self.arrived(3, far, 1)
        self.spread(2)

    def relay(self, qa):
        index = 4 + 4 * RING.index(qa)
        low, high = self.at.piece(qa, -1), self.at.piece(qa, 1)
        self.arrived(index, low)
        self.go(index + 2, low, self.at.device(0, 1), 0)
        self.arrived(index + 1, high)
        self.go(index + 3, high, self.at.device(0, -1), 1)
        self.to_sibling(qa, -1)
        self.to_sibling(qa, 1)

    def far(self, qa):
        index = 4 + 4 * RING.index(qa)
        piece = self.at.piece(qa, 2)
        self.arrived(index + 2, piece, 0)
        self.arrived(index + 3, piece, 1)
        self.to_sibling(qa, 2)

    def from_sibling(self, qa):
        for qb in RING:
            index = 20 + 4 * RING.index(qa) + RING.index(qb)
            self.arrived(index, self.at.piece(qa, qb, 1 - self.at.core))

    def own_group(self, qa):
        return [self.at.piece(qa, qb) for qb in RING]

    def sibling_group(self, qa):
        return [self.at.piece(qa, qb, 1 - self.at.core) for qb in RING]

    def steps(self):
        return [
            self.start,
            self.first_axis,
            self.first_axis_far,
            functools.partial(self.relay, 0),
            functools.partial(self.relay, -1),
            functools.partial(self.relay, 1),
            functools.partial(self.far, 0),
            functools.partial(self.relay, 2),
            functools.partial(self.far, -1),
            functools.partial(self.far, 1),
            functools.partial(self.far, 2),
        ]

    def finish(self):
        for descriptor in self.sent:
            descriptor.wait_send()


POSITION = {0: 0, 1: 1, 7: 2, 2: 3, 6: 4, 3: 5, 5: 6, 4: 7}
NEAR = 5
SIZE = (NEAR * 160, (8 - NEAR) * 160)
START = (0, SIZE[0])
PARTS = 4
CAP = 40


def kernel(
    attn_ref, context_ref, residual_ref, cot_ref, ids_ref, gates_ref, gain1_ref, wg_ref, wu_ref, wd_ref,
    og_ref, ou_ref, od_ref,
    rows_in0, rows_in1, rows_cot0, rows_cot1, ctx_all, wgu, wd, wtmp, acc0, acc1, back0, back1, ssq0, ssq1, dgu0, dgu1, hid0, hid1,
    part_gu, part_d, stage, gain_ref,
    red_in_l, red_in_s, red_out_l, red_out_s, red_sum, merged_all, attn_acc,
    res_all, cot_all, info_all, sel, route_x, route_c,
    w_sem, in0_send, in0_recv, in1_send, in1_recv, cot0_send, cot0_recv, cot1_send, cot1_recv,
    ctx_send, ctx_recv, in_local, ex_send, ex_recv, ex_local,
    rl_send, rl_recv, rs_send, rs_recv, ma_send, ma_recv, ga_send, ga_recv,
    tx_send, tx_recv, tc_send, tc_recv, out_sem,
):
    at = Coords()
    z, mp, dp = at.z, at.mp, at.dp
    own = at.piece(0, 0)
    hidden = wg_ref.shape[0]
    hid_pad = wgu.shape[0] // 2
    rows_in = (rows_in0, rows_in1)
    acc, acc_back, ssq, dgu, hid = (acc0, acc1), (back0, back1), (ssq0, ssq1), (dgu0, dgu1), (hid0, hid1)
    rows_cot = (rows_cot0, rows_cot1)
    pending = []

    def z_dev(k):
        return (lax.rem(z + k + 8, 8), mp, dp)

    def mp_dev(k):
        return (z, lax.rem(mp + k, 8), dp)

    def dp_dev(k):
        return (z, mp, lax.rem(dp + k, 4))

    def remote(src, dst, send, recv, device):
        return pltpu.make_async_remote_copy(
            src_ref=src, dst_ref=dst, send_sem=send, recv_sem=recv,
            device_id=device, device_id_type=MESH,
        )

    def push(src, dst, send, recv, device):
        descriptor = remote(src, dst, send, recv, device)
        descriptor.start()
        pending.append(descriptor)

    def landed(dst, recv, send):
        remote(dst, dst, send, recv, at.sibling()).wait_recv()

    barrier = pltpu.get_barrier_semaphore()
    peers = [z_dev(k) for k in range(1, 8)] + [mp_dev(k) for k in range(1, 8)]
    peers += [dp_dev(k) for k in range(1, 4)]
    for dy in (1, -1):
        y = lax.rem(at.y + dy + 4, 4)
        peers.append((z, lax.rem(y, 2) * 4 + at.x, lax.div(y, 2) * 2 + at.core))
    for peer in peers:
        pl.semaphore_signal(barrier, inc=1, device_id=peer, device_id_type=MESH)

    ctx_copy = pltpu.make_async_copy(context_ref, ctx_all.at[own], in_local.at[0])
    ctx_copy.start()
    dp_rows = pl.ds(pl.multiple_of(dp * 128, 128), 128)

    def columns(k):
        d = lax.rem(dp + k, 4)
        return pl.ds(pl.multiple_of(d * 1024 + mp * 128, 128), 128)

    locals_ = [
        pltpu.make_async_copy(residual_ref.at[:, columns(0)], res_all.at[dp_rows], ex_local.at[0]),
        pltpu.make_async_copy(cot_ref.at[:, columns(0)], cot_all.at[dp_rows], ex_local.at[1]),
    ]
    for copy in locals_:
        copy.start()

    gain_ref[...] = gain1_ref[...].astype(F32).reshape(32, 128)

    ids = ids_ref[...]
    experts = lax.broadcasted_iota(jnp.int32, (8, 128), 0)
    first = jnp.where(experts == ids[0:1, :], 1.0, 0.0)
    second = jnp.where(experts == ids[1:2, :], 1.0, 0.0)
    before = jnp.where(
        lax.broadcasted_iota(jnp.int32, (128, 128), 0) < lax.broadcasted_iota(jnp.int32, (128, 128), 1),
        1.0, 0.0,
    ).astype(BF)
    counts = jnp.dot(
        jnp.concatenate([first, second], axis=0).astype(BF), before, preferred_element_type=F32
    )
    slot0 = jnp.sum(first * counts[0:8], axis=0, keepdims=True)
    slot1 = jnp.sum(
        second * (counts[8:16] + jnp.sum(first, axis=1, keepdims=True)), axis=0, keepdims=True
    )
    base = (ids * 160 + dp * CAP).astype(F32)
    code0 = jnp.where(slot0 < CAP, base[0:1] + slot0, -1.0)
    code1 = jnp.where(slot1 < CAP, base[1:2] + slot1, -1.0)
    gates = gates_ref[...].astype(F32) / 32768.0
    info_all[dp] = jnp.concatenate([code0, code1, gates, jnp.zeros((4, 128), F32)], axis=0)
    pl.semaphore_wait(barrier, len(peers))

    for k in range(1, 4):
        push(cot_ref.at[:, columns(k)], cot_all.at[dp_rows], ex_send.at[0, k], ex_recv.at[0, k], dp_dev(k))
        push(info_all.at[dp], info_all.at[dp], ex_send.at[1, k], ex_recv.at[1, k], dp_dev(k))

    def chunk(k):
        t = lax.rem(z + k + 8, 8)
        return pl.ds(pl.multiple_of(t * 64, 64), 64)

    width = 1024 // PARTS
    part_cols = [pl.ds(h * width, width) for h in range(PARTS)]

    def reduce_step(step):
        for h in range(PARTS):
            cols = part_cols[h]
            sign = 1 - 2 * (h % 2)
            if step < 4:
                part = chunk(sign * (4 - step))
                src = attn_ref.at[part, cols]
                if step > 0:
                    landed(red_in_l.at[step - 1, h], rl_recv.at[step - 1, h], rl_send.at[step - 1, h])
                    red_out_l[step - 1, h] = (
                        red_in_l[step - 1, h].astype(F32) + attn_ref[part, cols].astype(F32)
                    ).astype(BF)
                    src = red_out_l.at[step - 1, h]
                push(src, red_in_l.at[step, h], rl_send.at[step, h], rl_recv.at[step, h], z_dev(sign))
            if step < 3:
                part = chunk(-sign * (3 - step))
                src = attn_ref.at[part, cols]
                if step > 0:
                    landed(red_in_s.at[step - 1, h], rs_recv.at[step - 1, h], rs_send.at[step - 1, h])
                    red_out_s[step - 1, h] = (
                        red_in_s[step - 1, h].astype(F32) + attn_ref[part, cols].astype(F32)
                    ).astype(BF)
                    src = red_out_s.at[step - 1, h]
                push(src, red_in_s.at[step, h], rs_send.at[step, h], rs_recv.at[step, h], z_dev(-sign))

    reduce_step(0)

    ctx_gather = PlaneGather(at, ctx_all, ctx_send, ctx_recv)
    cot_gather = (
        PlaneGather(at, rows_cot0, cot0_send, cot0_recv), PlaneGather(at, rows_cot1, cot1_send, cot1_recv)
    )
    in_gather = (
        PlaneGather(at, rows_in0, in0_send, in0_recv), PlaneGather(at, rows_in1, in1_send, in1_recv)
    )
    ctx_steps = ctx_gather.steps()
    cot_steps = [gather.steps() for gather in cot_gather]
    in_steps = [gather.steps() for gather in in_gather]

    def run(steps, count=1):
        for _ in range(count):
            if steps:
                steps.pop(0)()

    ctx_copy.wait()
    run(ctx_steps)

    weights = [
        pltpu.make_async_copy(wg_ref, wtmp.at[0], w_sem.at[0]),
        pltpu.make_async_copy(wu_ref, wtmp.at[1], w_sem.at[1]),
        pltpu.make_async_copy(wd_ref, wd, w_sem.at[2]),
    ]
    for copy in weights:
        copy.start()

    def from_group(k):
        d = lax.rem(dp - k + 4, 4)
        return pl.ds(pl.multiple_of(d * 128, 128), 128), d

    reduce_step(1)
    locals_[1].wait()
    for k in range(1, 4):
        rows, d = from_group(k)
        landed(cot_all.at[rows], ex_recv.at[0, k], ex_send.at[0, k])
        landed(info_all.at[d], ex_recv.at[1, k], ex_send.at[1, k])

    @pl.loop(0, 8)
    def _(e):
        place = (lax.broadcasted_iota(jnp.int32, (160, 128), 0) + e * 160).astype(F32)
        row_gate = jnp.zeros((160, 1), F32)
        rows = pl.ds(pl.multiple_of(e * 160, 160), 160)
        for d in range(4):
            info = info_all[d]
            first = place == info[0:1, :]
            second = place == info[1:2, :]
            sel[rows, d * 128:(d + 1) * 128] = jnp.where(first | second, 1.0, 0.0).astype(BF)
            gates = jnp.where(first, info[2:3, :], jnp.where(second, info[3:4, :], 0.0))
            row_gate += jnp.sum(gates, axis=1, keepdims=True)
        picked = jnp.dot(sel[rows, :], cot_all[...], preferred_element_type=F32)
        route_c[e] = (picked * row_gate).astype(BF)

    def block(k):
        place = POSITION[k]
        if place < NEAR:
            return 0, pl.ds(place * 160, 160)
        return 1, pl.ds((place - NEAR) * 160, 160)

    def exchange(route, gathered, send, recv, wanted):
        for k in sorted(range(1, 8), key=lambda k: POSITION[k]):
            half, rows = block(k)
            e = lax.rem(z - k + 8, 8)
            if half == wanted:
                push(route.at[e], gathered[half].at[own, rows], send.at[k], recv.at[k], z_dev(-k))
        if wanted == 0:
            half, rows = block(0)
            gathered[half][own, rows, :] = route[z]

    def exchanged(gathered, send, recv, wanted):
        for k in range(1, 8):
            half, rows = block(k)
            if half == wanted:
                landed(gathered[half].at[own, rows], recv.at[k], send.at[k])

    exchange(route_c, rows_cot, tc_send, tc_recv, 0)

    run(ctx_steps)
    reduce_step(2)
    for k in range(1, 4):
        push(residual_ref.at[:, columns(k)], res_all.at[dp_rows], ex_send.at[2, k], ex_recv.at[2, k], dp_dev(k))
    run(ctx_steps, 4)
    reduce_step(3)
    exchanged(rows_cot, tc_send, tc_recv, 0)
    run(cot_steps[0])
    run(ctx_steps, 3)

    for h in range(PARTS):
        landed(red_in_l.at[3, h], rl_recv.at[3, h], rl_send.at[3, h])
        landed(red_in_s.at[2, h], rs_recv.at[2, h], rs_send.at[2, h])
        total = (
            red_in_l[3, h].astype(F32) + red_in_s[2, h].astype(F32)
            + attn_ref[chunk(0), part_cols[h]].astype(F32)
        )
        mean = (total * 0.125).astype(BF)
        for part in range(8 // PARTS):
            red_sum[8 // PARTS * h + part] = mean[:, part * 128:(part + 1) * 128]
    exchange(route_c, rows_cot, tc_send, tc_recv, 1)
    own_rows = pl.ds(pl.multiple_of(z * 64, 64), 64)
    for k in range(1, 8):
        j = lax.rem(mp + k, 8)
        push(red_sum.at[j], merged_all.at[mp, own_rows], ma_send.at[k], ma_recv.at[k], mp_dev(k))
    merged_all[mp, own_rows, :] = red_sum[mp]
    run(cot_steps[0])
    for k in range(1, 8):
        j = lax.rem(mp - k + 8, 8)
        landed(merged_all.at[j, own_rows], ma_recv.at[k], ma_send.at[k])

    def merged_view(k, h):
        t = lax.rem(z + k + 8, 8)
        return merged_all.at[pl.ds(8 // PARTS * h, 8 // PARTS), pl.ds(pl.multiple_of(t * 64, 64), 64)]

    def gather_step(step):
        for h in range(PARTS):
            sign = 1 - 2 * (h % 2)
            if step > 0:
                landed(merged_view(-sign * step, h), ga_recv.at[0, step - 1, h], ga_send.at[0, step - 1, h])
            if step < 4:
                view = merged_view(-sign * step, h)
                push(view, view, ga_send.at[0, step, h], ga_recv.at[0, step, h], z_dev(sign))
            if 0 < step < 4:
                landed(merged_view(sign * step, h), ga_recv.at[1, step - 1, h], ga_send.at[1, step - 1, h])
            if step < 3:
                view = merged_view(sign * step, h)
                push(view, view, ga_send.at[1, step, h], ga_recv.at[1, step, h], z_dev(-sign))

    gather_step(0)
    run(ctx_steps, 2)
    run(cot_steps[0], 2)
    exchanged(rows_cot, tc_send, tc_recv, 1)
    run(cot_steps[1])
    gather_step(1)
    run(cot_steps[0], 2)
    gather_step(2)
    run(cot_steps[1])
    run(cot_steps[0])
    gather_step(3)
    run(cot_steps[0], 2)
    run(cot_steps[1])
    gather_step(4)
    for qa in RING:
        ctx_gather.from_sibling(qa)
    for k in range(1, 4):
        rows, _ = from_group(k)
        landed(res_all.at[rows], ex_recv.at[2, k], ex_send.at[2, k])
    locals_[0].wait()

    def lanes(piece):
        return pl.ds(pl.multiple_of(piece * 128, 128), 128)

    def gain_of(piece):
        return gain_ref[pl.ds(piece, 1), :]

    for j in range(8):
        context = jnp.concatenate([ctx_all[d * 8 + j] for d in range(4)], axis=0)
        product = jnp.dot(context, merged_all[j], preferred_element_type=F32)
        if j == 0:
            attn_acc[...] = product + res_all[...].astype(F32)
        else:
            attn_acc[...] += product
    res_all[...] = (attn_acc[...] * gain_of(own)).astype(BF)

    @pl.loop(0, 8)
    def _(e):
        rows = pl.ds(pl.multiple_of(e * 160, 160), 160)
        route_x[e] = jnp.dot(sel[rows, :], res_all[...], preferred_element_type=F32).astype(BF)

    exchange(route_x, rows_in, tx_send, tx_recv, 0)

    for copy in weights:
        copy.wait()
    wgu[0:hidden, :] = wtmp[0]
    wgu[hid_pad:hid_pad + hidden, :] = wtmp[1]
    for ref in acc + acc_back + ssq:
        ref[...] = jnp.zeros_like(ref)

    def tiles(half):
        return [(start, min(256, SIZE[half] - start)) for start in range(0, SIZE[half], 256)]

    def back_group(half, group):
        lhs = jnp.concatenate([wd[:, lanes(p)] for p in group], axis=1)
        for start, width in tiles(half):
            rhs = jnp.concatenate([rows_cot[half][p, start:start + width, :] for p in group], axis=1)
            cols = slice(start, start + width)
            acc_back[half][:, cols] += lax.dot_general(lhs, rhs, NT, preferred_element_type=F32)

    def fore_group(half, group):
        lhs = jnp.concatenate([wgu[:, lanes(p)] for p in group], axis=1)
        inverse = [1.0 / gain_of(p) for p in group]
        for start, width in tiles(half):
            parts = [rows_in[half][p, start:start + width, :] for p in group]
            cols = slice(start, start + width)
            acc[half][:, cols] += lax.dot_general(
                lhs, jnp.concatenate(parts, axis=1), NT, preferred_element_type=F32
            )
            squares = ssq[half][cols, :]
            for part, scale in zip(parts, inverse):
                value = part.astype(F32) * scale
                squares += value * value
            ssq[half][cols, :] = squares

    def own_back(half, *places):
        for qa in places:
            back_group(half, cot_gather[half].own_group(qa))

    def sibling_back(half, *places):
        for qa in places:
            cot_gather[half].from_sibling(qa)
            back_group(half, cot_gather[half].sibling_group(qa))

    def own_fore(half, *places):
        for qa in places:
            fore_group(half, in_gather[half].own_group(qa))

    def sibling_fore(half, *places):
        for qa in places:
            in_gather[half].from_sibling(qa)
            fore_group(half, in_gather[half].sibling_group(qa))

    def activations(half):
        for start in range(0, SIZE[half], 128):
            cols = slice(start, min(start + 128, SIZE[half]))
            squares = lax.dot_general(
                jnp.ones((8, 128), BF), ssq[half][cols, :].astype(BF), NT, preferred_element_type=F32
            )
            inv = lax.rsqrt(squares[0:1] * (1.0 / 4096.0) + 1e-05)
            gate = acc[half][0:hidden, cols] * inv
            up = acc[half][hid_pad:hid_pad + hidden, cols] * inv
            back = acc_back[half][:, cols]
            sig = jax.nn.sigmoid(gate)
            active = gate * sig
            hid[half][:, cols] = (active * up).astype(BF)
            back = back * inv
            dgu[half][0:hidden, cols] = (back * up * sig * (1.0 + gate * (1.0 - sig))).astype(BF)
            dgu[half][hid_pad:hid_pad + hidden, cols] = (back * active).astype(BF)

    def gradients(half, chunk):
        @pl.loop(0, 4)
        def _(i):
            n = chunk * 4 + i
            cols = pl.ds(pl.multiple_of(n * 256, 256), 256)
            rhs = jnp.concatenate([rows_in[half][2 * n], rows_in[half][2 * n + 1]], axis=1)
            both = jnp.dot(dgu[half][...], rhs, preferred_element_type=F32)
            rhs = jnp.concatenate([rows_cot[half][2 * n], rows_cot[half][2 * n + 1]], axis=1)
            down = jnp.dot(hid[half][...], rhs, preferred_element_type=F32)
            if half == 0:
                part_gu[:, cols] = both
                part_d[:, cols] = down
            else:
                both = (both + part_gu[:, cols]).astype(BF)
                stage[0, :, cols] = both[0:hidden]
                stage[1, :, cols] = both[hid_pad:hid_pad + hidden]
                stage[2, :, cols] = (down + part_d[:, cols]).astype(BF)

    run(cot_steps[1], 2)
    run(cot_steps[0], 3)
    run(cot_steps[1], 1)
    exchanged(rows_in, tx_send, tx_recv, 0)
    exchange(route_x, rows_in, tx_send, tx_recv, 1)
    run(in_steps[0])
    run(cot_steps[1], 2)
    own_back(0, 0, -1, 1, 2)
    run(cot_steps[1], 2)
    run(in_steps[0])
    run(cot_steps[1], 1)
    sibling_back(0, 0, -1)
    run(in_steps[0])
    sibling_back(0, 1, 2)
    run(in_steps[0], 3)
    own_back(1, 0, -1, 1, 2)
    exchanged(rows_in, tx_send, tx_recv, 1)
    run(in_steps[1])
    sibling_back(1, 0, -1, 1, 2)
    run(in_steps[0], 2)
    own_fore(0, 0)
    run(in_steps[1])
    run(in_steps[0])
    own_fore(0, -1)
    run(in_steps[0])
    own_fore(0, 1)
    run(in_steps[1])
    sibling_fore(0, 0)
    run(in_steps[0])
    own_fore(0, 2)
    run(in_steps[1])
    sibling_fore(0, -1, 1)
    run(in_steps[1], 2)
    sibling_fore(0, 2)
    run(in_steps[1], 2)
    activations(0)
    gradients(0, 0)
    run(in_steps[1])
    gradients(0, 1)
    run(in_steps[1])
    gradients(0, 2)
    run(in_steps[1])
    gradients(0, 3)
    while in_steps[1]:
        run(in_steps[1])
    own_fore(1, 0, -1, 1, 2)
    sibling_fore(1, 0, -1, 1, 2)
    activations(1)
    outs = (og_ref, ou_ref, od_ref)
    writes = []
    for quarter in range(4):
        gradients(1, quarter)
        cols = pl.ds(quarter * 1024, 1024)
        for index in range(3):
            write = pltpu.make_async_copy(
                stage.at[index, :, cols], outs[index].at[:, cols], out_sem.at[index, quarter]
            )
            write.start()
            writes.append(write)

    assert not any([ctx_steps] + cot_steps + in_steps)
    for gather in (ctx_gather,) + cot_gather + in_gather:
        gather.finish()
    for descriptor in pending:
        descriptor.wait_send()
    for write in writes:
        write.wait()


def write_kernel(*refs):
    count = 3
    sources, outs, hold, sem_in, sem_out = refs[:count], refs[count:2 * count], *refs[2 * count:]
    reads, writes = [], []
    for index in range(count):
        for part in range(4):
            cols = pl.ds(part * 1024, 1024)
            there = hold.at[index, :, cols]
            reads.append(pltpu.make_async_copy(sources[index].at[:, cols], there, sem_in.at[index, part]))
            writes.append(pltpu.make_async_copy(there, outs[index].at[:, cols], sem_out.at[index, part]))
    for read in reads:
        read.start()
    for read, write in zip(reads, writes):
        read.wait()
        write.start()
    for write in writes:
        write.wait()


def per_device(
    context, residual, attn_weight, norm_gain, gate_weight, up_weight, down_weight,
    cotangent, expert_ids, gate_fixed,
):
    hidden = gate_weight.shape[2]
    pad = 176
    dma = pltpu.SemaphoreType.DMA
    vmem = pl.BlockSpec(memory_space=pltpu.VMEM)
    hbm = pl.BlockSpec(memory_space=pl.ANY)
    out = jax.ShapeDtypeStruct((hidden, 4096), BF)
    copies = PlaneGather.COPIES
    near, far = SIZE
    grads = pl.pallas_call(
        kernel,
        out_shape=(out, out, out),
        in_specs=[vmem, hbm, hbm, hbm, vmem, vmem, vmem, hbm, hbm, hbm],
        out_specs=(hbm, hbm, hbm),
        scratch_shapes=[
            pltpu.VMEM((32, near, 128), BF),
            pltpu.VMEM((32, far, 128), BF),
            pltpu.VMEM((32, near, 128), BF),
            pltpu.VMEM((32, far, 128), BF),
            pltpu.VMEM((32, 128, 512), BF),
            pltpu.VMEM((2 * pad, 4096), BF),
            pltpu.VMEM((hidden, 4096), BF),
            pltpu.VMEM((2, hidden, 4096), BF),
            pltpu.VMEM((2 * pad, near), F32),
            pltpu.VMEM((2 * pad, far), F32),
            pltpu.VMEM((hidden, near), F32),
            pltpu.VMEM((hidden, far), F32),
            pltpu.VMEM((near, 128), F32),
            pltpu.VMEM((far, 128), F32),
            pltpu.VMEM((2 * pad, near), BF),
            pltpu.VMEM((2 * pad, far), BF),
            pltpu.VMEM((hidden, near), BF),
            pltpu.VMEM((hidden, far), BF),
            pltpu.VMEM((2 * pad, 4096), F32),
            pltpu.VMEM((hidden, 4096), F32),
            pltpu.VMEM((3, hidden, 4096), BF),
            pltpu.VMEM((32, 128), F32),
            pltpu.VMEM((4, PARTS, 64, 1024 // PARTS), BF),
            pltpu.VMEM((3, PARTS, 64, 1024 // PARTS), BF),
            pltpu.VMEM((3, PARTS, 64, 1024 // PARTS), BF),
            pltpu.VMEM((2, PARTS, 64, 1024 // PARTS), BF),
            pltpu.VMEM((8, 64, 128), BF),
            pltpu.VMEM((8, 512, 128), BF),
            pltpu.VMEM((512, 128), F32),
            pltpu.VMEM((512, 128), BF),
            pltpu.VMEM((512, 128), BF),
            pltpu.VMEM((4, 8, 128), F32),
            pltpu.VMEM((1280, 512), BF),
            pltpu.VMEM((8, 160, 128), BF),
            pltpu.VMEM((8, 160, 128), BF),
            dma((3,)),
            dma((copies,)), dma((copies,)), dma((copies,)), dma((copies,)),
            dma((copies,)), dma((copies,)), dma((copies,)), dma((copies,)),
            dma((copies,)), dma((copies,)), dma((1,)),
            dma((3, 4)), dma((3, 4)), dma((2,)),
            dma((4, PARTS)), dma((4, PARTS)), dma((3, PARTS)), dma((3, PARTS)),
            dma((8,)), dma((8,)),
            dma((2, 4, PARTS)), dma((2, 4, PARTS)),
            dma((8,)), dma((8,)),
            dma((8,)), dma((8,)),
            dma((3, 4)),
        ],
        compiler_params=pltpu.CompilerParams(
            collective_id=0, has_side_effects=True, vmem_limit_bytes=67_000_000
        ),
    )(
        attn_weight[0], context, residual, cotangent, expert_ids.T, gate_fixed.T, norm_gain,
        gate_weight[0].T, up_weight[0].T, down_weight[0],
    )
    grads = pl.pallas_call(
        write_kernel,
        out_shape=(out, out, out),
        in_specs=[hbm, hbm, hbm],
        out_specs=(hbm, hbm, hbm),
        scratch_shapes=[pltpu.VMEM((3, hidden, 4096), BF), dma((3, 4)), dma((3, 4))],
    )(*grads)
    return grads[0].T[None], grads[1].T[None], grads[2][None]


def solution(mesh):
    return jax.shard_map(
        per_device,
        mesh=mesh,
        in_specs=(
            P(("branch", "dp"), "mp"),
            P(("branch", "dp"), None),
            P("branch", "mp", "dp"),
            P(),
            P("branch", None, ("mp", "dp")),
            P("branch", None, ("mp", "dp")),
            P("branch", ("mp", "dp"), None),
            P(("branch", "dp"), None),
            P(("branch", "dp"), None),
            P(("branch", "dp"), None),
        ),
        out_specs=(
            P("branch", None, ("mp", "dp")),
            P("branch", None, ("mp", "dp")),
            P("branch", ("mp", "dp"), None),
        ),
        check_vma=False,
    )
```

```python
import functools

import jax
import jax.numpy as jnp
from jax import lax
from jax.experimental import pallas as pl
from jax.experimental.pallas import tpu as pltpu
from jax.sharding import PartitionSpec as P

MESH = pl.DeviceIdType.MESH
BF = jnp.bfloat16
F32 = jnp.float32
NT = (((1,), (1,)), ((), ()))


class Coords:
    def __init__(self):
        self.z = lax.axis_index("branch")
        self.mp = lax.axis_index("mp")
        self.dp = lax.axis_index("dp")
        self.x = lax.rem(self.mp, 4)
        self.core = lax.rem(self.dp, 2)
        self.y = lax.div(self.dp, 2) * 2 + lax.div(self.mp, 4)

    def at(self, da, db, core):
        other = 1 - core
        x = lax.rem(self.x + other * da + core * db + 8, 4)
        y = lax.rem(self.y + core * da + other * db + 8, 4)
        return x, y

    def device(self, da, db):
        x, y = self.at(da, db, self.core)
        return (self.z, lax.rem(y, 2) * 4 + x, lax.div(y, 2) * 2 + self.core)

    def piece(self, da, db, core=None):
        core = self.core if core is None else core
        x, y = self.at(da, db, core)
        return (lax.div(y, 2) * 2 + core) * 8 + lax.rem(y, 2) * 4 + x

    def sibling(self):
        return (self.z, self.mp, self.dp + 1 - 2 * self.core)


RING = (0, -1, 1, 2)


class PlaneGather:
    COPIES = 36

    def __init__(self, at, buf, send, recv, start=0, size=None):
        self.at, self.buf, self.send, self.recv = at, buf, send, recv
        self.base, self.size = start, buf.shape[1] if size is None else size
        self.half = self.size // 2
        self.sent = []

    def view(self, piece, half=None):
        if half is None:
            return self.buf.at[piece, pl.ds(self.base, self.size)]
        return self.buf.at[piece, pl.ds(self.base + half * self.half, self.half)]

    def copy(self, index, piece, device, half=None):
        ref = self.view(piece, half)
        return pltpu.make_async_remote_copy(
            src_ref=ref,
            dst_ref=ref,
            send_sem=self.send.at[index],
            recv_sem=self.recv.at[index],
            device_id=device,
            device_id_type=MESH,
        )

    def go(self, index, piece, device, half=None):
        descriptor = self.copy(index, piece, device, half)
        descriptor.start()
        self.sent.append(descriptor)

    def arrived(self, index, piece, half=None):
        self.copy(index, piece, self.at.sibling(), half).wait_recv()

    def to_sibling(self, qa, qb):
        index = 20 + 4 * RING.index(qa) + RING.index(qb)
        self.go(index, self.at.piece(qa, qb), self.at.sibling())

    def spread(self, qa):
        index = 4 + 4 * RING.index(qa)
        piece = self.at.piece(qa, 0)
        self.go(index, piece, self.at.device(0, 1))
        self.go(index + 1, piece, self.at.device(0, -1))
        self.to_sibling(qa, 0)

    def start(self):
        piece = self.at.piece(0, 0)
        self.go(0, piece, self.at.device(1, 0))
        self.go(1, piece, self.at.device(-1, 0))
        self.spread(0)

    def first_axis(self):
        low, high = self.at.piece(-1, 0), self.at.piece(1, 0)
        self.arrived(0, low)
        self.go(2, low, self.at.device(1, 0), 0)
        self.arrived(1, high)
        self.go(3, high, self.at.device(-1, 0), 1)
        self.spread(-1)
        self.spread(1)

    def first_axis_far(self):
        far = self.at.piece(2, 0)
        self.arrived(2, far, 0)
        self.arrived(3, far, 1)
        self.spread(2)

    def relay(self, qa):
        index = 4 + 4 * RING.index(qa)
        low, high = self.at.piece(qa, -1), self.at.piece(qa, 1)
        self.arrived(index, low)
        self.go(index + 2, low, self.at.device(0, 1), 0)
        self.arrived(index + 1, high)
        self.go(index + 3, high, self.at.device(0, -1), 1)
        self.to_sibling(qa, -1)
        self.to_sibling(qa, 1)

    def far(self, qa):
        index = 4 + 4 * RING.index(qa)
        piece = self.at.piece(qa, 2)
        self.arrived(index + 2, piece, 0)
        self.arrived(index + 3, piece, 1)
        self.to_sibling(qa, 2)

    def from_sibling(self, qa):
        for qb in RING:
            index = 20 + 4 * RING.index(qa) + RING.index(qb)
            self.arrived(index, self.at.piece(qa, qb, 1 - self.at.core))

    def own_group(self, qa):
        return [self.at.piece(qa, qb) for qb in RING]

    def sibling_group(self, qa):
        return [self.at.piece(qa, qb, 1 - self.at.core) for qb in RING]

    def steps(self):
        return [
            self.start,
            self.first_axis,
            self.first_axis_far,
            functools.partial(self.relay, 0),
            functools.partial(self.relay, -1),
            functools.partial(self.relay, 1),
            functools.partial(self.relay, 2),
            functools.partial(self.far, 0),
            functools.partial(self.far, -1),
            functools.partial(self.far, 1),
            functools.partial(self.far, 2),
        ]

    def finish(self):
        for descriptor in self.sent:
            descriptor.wait_send()


POSITION = {0: 0, 1: 1, 7: 2, 2: 3, 6: 4, 3: 5, 5: 6, 4: 7}
NEAR = 5
SIZE = (NEAR * 160, (8 - NEAR) * 160)
WHOLE = SIZE[0] // 256 * 256
LEFT = SIZE[0] - WHOLE
PARTS = 4
CAP = 40


def kernel(
    attn_hbm, context_ref, residual_ref, cot_ref, ids_ref, gates_ref, gain1_ref, wg_ref, wu_ref, wd_ref,
    og_ref, ou_ref, od_ref,
    rows_in0, rows_in1, rows_cot0, rows_cot1, ctx_all, wgu, wd, wtmp, acc0, acc1, back0, back1, ssq0, ssq1, dgu0, dgu1, hid0, hid1,
    part_gu, part_d, stage, gain_ref, attn_ref,
    red_in_l, red_in_s, red_out_l, red_out_s, red_sum, merged_all, attn_acc,
    res_all, cot_all, info_all, sel, route_x, route_c,
    w_sem, in0_send, in0_recv, in1_send, in1_recv,
    cotz_send, cotz_recv, cot0_send, cot0_recv, cot1_send, cot1_recv,
    ctx_send, ctx_recv, in_local, ex_send, ex_recv, ex_local,
    rl_send, rl_recv, rs_send, rs_recv, ma_send, ma_recv, ga_send, ga_recv,
    tx_send, tx_recv, tc_send, tc_recv, out_sem,
):
    at = Coords()
    z, mp, dp = at.z, at.mp, at.dp
    own = at.piece(0, 0)
    hidden = wg_ref.shape[0]
    hid_pad = wgu.shape[0] // 2
    rows_in = (rows_in0, rows_in1)
    acc, acc_back, ssq, dgu, hid = (acc0, acc1), (back0, back1), (ssq0, ssq1), (dgu0, dgu1), (hid0, hid1)
    rows_cot = (rows_cot0, rows_cot1)
    pending = []

    def z_dev(k):
        return (lax.rem(z + k + 8, 8), mp, dp)

    def mp_dev(k):
        return (z, lax.rem(mp + k, 8), dp)

    def dp_dev(k):
        return (z, mp, lax.rem(dp + k, 4))

    def remote(src, dst, send, recv, device):
        return pltpu.make_async_remote_copy(
            src_ref=src, dst_ref=dst, send_sem=send, recv_sem=recv,
            device_id=device, device_id_type=MESH,
        )

    def push(src, dst, send, recv, device):
        descriptor = remote(src, dst, send, recv, device)
        descriptor.start()
        pending.append(descriptor)

    def landed(dst, recv, send):
        remote(dst, dst, send, recv, at.sibling()).wait_recv()

    barrier = pltpu.get_barrier_semaphore()
    peers = [z_dev(k) for k in range(1, 8)] + [mp_dev(k) for k in range(1, 8)]
    peers += [dp_dev(k) for k in range(1, 4)]
    for dy in (1, -1):
        y = lax.rem(at.y + dy + 4, 4)
        peers.append((z, lax.rem(y, 2) * 4 + at.x, lax.div(y, 2) * 2 + at.core))
    for peer in peers:
        pl.semaphore_signal(barrier, inc=1, device_id=peer, device_id_type=MESH)

    ctx_copy = pltpu.make_async_copy(context_ref, ctx_all.at[own], in_local.at[0])
    ctx_copy.start()
    dp_rows = pl.ds(pl.multiple_of(dp * 128, 128), 128)

    def columns(k):
        d = lax.rem(dp + k, 4)
        return pl.ds(pl.multiple_of(d * 1024 + mp * 128, 128), 128)

    locals_ = [
        pltpu.make_async_copy(residual_ref.at[:, columns(0)], res_all.at[dp_rows], ex_local.at[0]),
        pltpu.make_async_copy(cot_ref.at[:, columns(0)], cot_all.at[dp_rows], ex_local.at[1]),
    ]
    attn_copy = pltpu.make_async_copy(attn_hbm, attn_ref, in_local.at[1])
    attn_copy.start()
    for copy in locals_:
        copy.start()

    gain_ref[...] = gain1_ref[...].astype(F32).reshape(32, 128)

    ids = ids_ref[...]
    experts = lax.broadcasted_iota(jnp.int32, (8, 128), 0)
    first = jnp.where(experts == ids[0:1, :], 1.0, 0.0)
    second = jnp.where(experts == ids[1:2, :], 1.0, 0.0)
    before = jnp.where(
        lax.broadcasted_iota(jnp.int32, (128, 128), 0) < lax.broadcasted_iota(jnp.int32, (128, 128), 1),
        1.0, 0.0,
    ).astype(BF)
    counts = jnp.dot(
        jnp.concatenate([first, second], axis=0).astype(BF), before, preferred_element_type=F32
    )
    slot0 = jnp.sum(first * counts[0:8], axis=0, keepdims=True)
    slot1 = jnp.sum(
        second * (counts[8:16] + jnp.sum(first, axis=1, keepdims=True)), axis=0, keepdims=True
    )
    base = (ids * 160 + dp * CAP).astype(F32)
    code0 = jnp.where(slot0 < CAP, base[0:1] + slot0, -1.0)
    code1 = jnp.where(slot1 < CAP, base[1:2] + slot1, -1.0)
    gates = gates_ref[...].astype(F32) / 32768.0
    info_all[dp] = jnp.concatenate([code0, code1, gates, jnp.zeros((4, 128), F32)], axis=0)
    pl.semaphore_wait(barrier, len(peers))

    for k in range(1, 4):
        push(cot_ref.at[:, columns(k)], cot_all.at[dp_rows], ex_send.at[0, k], ex_recv.at[0, k], dp_dev(k))
        push(info_all.at[dp], info_all.at[dp], ex_send.at[1, k], ex_recv.at[1, k], dp_dev(k))

    def chunk(k):
        t = lax.rem(z + k + 8, 8)
        return pl.ds(pl.multiple_of(t * 64, 64), 64)

    width = 1024 // PARTS
    part_cols = [pl.ds(h * width, width) for h in range(PARTS)]

    def reduce_step(step):
        for h in range(PARTS):
            cols = part_cols[h]
            sign = 1 - 2 * (h % 2)
            if step < 4:
                part = chunk(sign * (4 - step))
                src = attn_hbm.at[part, cols]
                if step > 0:
                    landed(red_in_l.at[step - 1, h], rl_recv.at[step - 1, h], rl_send.at[step - 1, h])
                    red_out_l[step - 1, h] = (
                        red_in_l[step - 1, h].astype(F32) + attn_ref[part, cols].astype(F32)
                    ).astype(BF)
                    src = red_out_l.at[step - 1, h]
                push(src, red_in_l.at[step, h], rl_send.at[step, h], rl_recv.at[step, h], z_dev(sign))
            if step < 3:
                part = chunk(-sign * (3 - step))
                src = attn_hbm.at[part, cols]
                if step > 0:
                    landed(red_in_s.at[step - 1, h], rs_recv.at[step - 1, h], rs_send.at[step - 1, h])
                    red_out_s[step - 1, h] = (
                        red_in_s[step - 1, h].astype(F32) + attn_ref[part, cols].astype(F32)
                    ).astype(BF)
                    src = red_out_s.at[step - 1, h]
                push(src, red_in_s.at[step, h], rs_send.at[step, h], rs_recv.at[step, h], z_dev(-sign))

    reduce_step(0)

    ctx_gather = PlaneGather(at, ctx_all, ctx_send, ctx_recv)
    rest = SIZE[0] - 160
    cot_gather = (
        PlaneGather(at, rows_cot0, cot0_send, cot0_recv, 160, rest),
        PlaneGather(at, rows_cot1, cot1_send, cot1_recv),
        PlaneGather(at, rows_cot0, cotz_send, cotz_recv, 0, 160),
    )
    in_gather = (
        PlaneGather(at, rows_in0, in0_send, in0_recv),
        PlaneGather(at, rows_in1, in1_send, in1_recv),
    )
    ctx_steps = ctx_gather.steps()
    cot_steps = [gather.steps() for gather in cot_gather]
    in_steps = [gather.steps() for gather in in_gather]

    def run(steps, count=1):
        for _ in range(count):
            if steps:
                steps.pop(0)()

    ctx_copy.wait()
    run(ctx_steps)

    weights = [
        pltpu.make_async_copy(wg_ref, wtmp.at[0], w_sem.at[0]),
        pltpu.make_async_copy(wu_ref, wtmp.at[1], w_sem.at[1]),
        pltpu.make_async_copy(wd_ref, wd, w_sem.at[2]),
    ]
    for copy in weights:
        copy.start()

    def from_group(k):
        d = lax.rem(dp - k + 4, 4)
        return pl.ds(pl.multiple_of(d * 128, 128), 128), d

    attn_copy.wait()
    reduce_step(1)
    locals_[1].wait()
    for k in range(1, 4):
        rows, d = from_group(k)
        landed(cot_all.at[rows], ex_recv.at[0, k], ex_send.at[0, k])
        landed(info_all.at[d], ex_recv.at[1, k], ex_send.at[1, k])

    @pl.loop(0, 8)
    def _(e):
        place = (lax.broadcasted_iota(jnp.int32, (160, 128), 0) + e * 160).astype(F32)
        row_gate = jnp.zeros((160, 1), F32)
        rows = pl.ds(pl.multiple_of(e * 160, 160), 160)
        for d in range(4):
            info = info_all[d]
            first = place == info[0:1, :]
            second = place == info[1:2, :]
            sel[rows, d * 128:(d + 1) * 128] = jnp.where(first | second, 1.0, 0.0).astype(BF)
            gates = jnp.where(first, info[2:3, :], jnp.where(second, info[3:4, :], 0.0))
            row_gate += jnp.sum(gates, axis=1, keepdims=True)
        picked = jnp.dot(sel[rows, :], cot_all[...], preferred_element_type=F32)
        route_c[e] = (picked * row_gate).astype(BF)

    def block(k):
        place = POSITION[k]
        if place < NEAR:
            return 0, pl.ds(place * 160, 160)
        return 1, pl.ds((place - NEAR) * 160, 160)

    def exchange(route, gathered, send, recv, wanted):
        if wanted == 0:
            half, rows = block(0)
            gathered[half][own, rows, :] = route[z]
        for k in sorted(range(1, 8), key=lambda k: POSITION[k]):
            half, rows = block(k)
            e = lax.rem(z - k + 8, 8)
            if half == wanted:
                push(route.at[e], gathered[half].at[own, rows], send.at[k], recv.at[k], z_dev(-k))

    def exchanged(gathered, send, recv, wanted):
        for k in range(1, 8):
            half, rows = block(k)
            if half == wanted:
                landed(gathered[half].at[own, rows], recv.at[k], send.at[k])

    cot_near, cot_far, cot_own = cot_steps
    in_near, in_far = in_steps
    run(ctx_steps)
    reduce_step(2)
    exchange(route_c, rows_cot, tc_send, tc_recv, 0)
    run(cot_own)
    for k in range(1, 4):
        push(residual_ref.at[:, columns(k)], res_all.at[dp_rows], ex_send.at[2, k], ex_recv.at[2, k], dp_dev(k))
    run(ctx_steps, 2)
    reduce_step(3)
    run(cot_own)
    run(ctx_steps, 2)

    for h in range(PARTS):
        landed(red_in_l.at[3, h], rl_recv.at[3, h], rl_send.at[3, h])
        landed(red_in_s.at[2, h], rs_recv.at[2, h], rs_send.at[2, h])
        total = (
            red_in_l[3, h].astype(F32) + red_in_s[2, h].astype(F32)
            + attn_ref[chunk(0), part_cols[h]].astype(F32)
        )
        mean = (total * 0.125).astype(BF)
        for part in range(8 // PARTS):
            red_sum[8 // PARTS * h + part] = mean[:, part * 128:(part + 1) * 128]
    own_rows = pl.ds(pl.multiple_of(z * 64, 64), 64)
    for k in range(1, 8):
        j = lax.rem(mp + k, 8)
        push(red_sum.at[j], merged_all.at[mp, own_rows], ma_send.at[k], ma_recv.at[k], mp_dev(k))
    merged_all[mp, own_rows, :] = red_sum[mp]
    exchange(route_c, rows_cot, tc_send, tc_recv, 1)
    exchanged(rows_cot, tc_send, tc_recv, 0)
    run(cot_near)
    run(ctx_steps)
    run(cot_own, 2)
    for k in range(1, 8):
        j = lax.rem(mp - k + 8, 8)
        landed(merged_all.at[j, own_rows], ma_recv.at[k], ma_send.at[k])

    def merged_view(k, h):
        t = lax.rem(z + k + 8, 8)
        return merged_all.at[pl.ds(8 // PARTS * h, 8 // PARTS), pl.ds(pl.multiple_of(t * 64, 64), 64)]

    def gather_step(step):
        for h in range(PARTS):
            sign = 1 - 2 * (h % 2)
            if step > 0:
                landed(merged_view(-sign * step, h), ga_recv.at[0, step - 1, h], ga_send.at[0, step - 1, h])
            if step < 4:
                view = merged_view(-sign * step, h)
                push(view, view, ga_send.at[0, step, h], ga_recv.at[0, step, h], z_dev(sign))
            if 0 < step < 4:
                landed(merged_view(sign * step, h), ga_recv.at[1, step - 1, h], ga_send.at[1, step - 1, h])
            if step < 3:
                view = merged_view(sign * step, h)
                push(view, view, ga_send.at[1, step, h], ga_recv.at[1, step, h], z_dev(-sign))

    gather_step(0)
    run(ctx_steps, 2)
    run(cot_own, 2)
    run(cot_near)
    gather_step(1)
    run(cot_near, 2)
    exchanged(rows_cot, tc_send, tc_recv, 1)
    run(cot_far)
    run(ctx_steps, 2)
    gather_step(2)
    run(cot_near, 2)
    run(cot_own)
    gather_step(3)
    run(cot_far)
    run(cot_near)
    gather_step(4)
    for qa in RING:
        ctx_gather.from_sibling(qa)
    for k in range(1, 4):
        rows, _ = from_group(k)
        landed(res_all.at[rows], ex_recv.at[2, k], ex_send.at[2, k])
    locals_[0].wait()

    def lanes(piece):
        return pl.ds(pl.multiple_of(piece * 128, 128), 128)

    def gain_of(piece):
        return gain_ref[pl.ds(piece, 1), :]

    for j in range(8):
        context = jnp.concatenate([ctx_all[d * 8 + j] for d in range(4)], axis=0)
        product = jnp.dot(context, merged_all[j], preferred_element_type=F32)
        if j == 0:
            attn_acc[...] = product + res_all[...].astype(F32)
        else:
            attn_acc[...] += product
    res_all[...] = (attn_acc[...] * gain_of(own)).astype(BF)

    @pl.loop(0, 8)
    def _(e):
        rows = pl.ds(pl.multiple_of(e * 160, 160), 160)
        route_x[e] = jnp.dot(sel[rows, :], res_all[...], preferred_element_type=F32).astype(BF)

    exchange(route_x, rows_in, tx_send, tx_recv, 0)

    for copy in weights:
        copy.wait()
    wgu[0:hidden, :] = wtmp[0]
    wgu[hid_pad:hid_pad + hidden, :] = wtmp[1]
    for ref in acc + acc_back + ssq:
        ref[...] = jnp.zeros_like(ref)

    def tiles(half):
        return [(start, min(256, SIZE[half] - start)) for start in range(0, SIZE[half], 256)]

    def back_group(half, group):
        lhs = jnp.concatenate([wd[:, lanes(p)] for p in group], axis=1)
        for start, width in tiles(half):
            rhs = jnp.concatenate([rows_cot[half][p, start:start + width, :] for p in group], axis=1)
            cols = slice(start, start + width)
            acc_back[half][:, cols] += lax.dot_general(lhs, rhs, NT, preferred_element_type=F32)

    def fore_group(half, group):
        lhs = jnp.concatenate([wgu[:, lanes(p)] for p in group], axis=1)
        inverse = [1.0 / gain_of(p) for p in group]
        for start, width in tiles(half):
            parts = [rows_in[half][p, start:start + width, :] for p in group]
            cols = slice(start, start + width)
            acc[half][:, cols] += lax.dot_general(
                lhs, jnp.concatenate(parts, axis=1), NT, preferred_element_type=F32
            )
            squares = ssq[half][cols, :]
            for part, scale in zip(parts, inverse):
                value = part.astype(F32) * scale
                squares += value * value
            ssq[half][cols, :] = squares

    def own_back(half, *places):
        for qa in places:
            back_group(half, cot_gather[half].own_group(qa))

    def sibling_back(half, *places):
        for qa in places:
            if half == 0:
                cot_gather[2].from_sibling(qa)
            cot_gather[half].from_sibling(qa)
            back_group(half, cot_gather[half].sibling_group(qa))

    def own_fore(half, *places):
        for qa in places:
            fore_group(half, in_gather[half].own_group(qa))

    def sibling_fore(half, *places):
        for qa in places:
            in_gather[half].from_sibling(qa)
            fore_group(half, in_gather[half].sibling_group(qa))

    def activations(half):
        for start in range(0, SIZE[half], 128):
            cols = slice(start, min(start + 128, SIZE[half]))
            into, place = half, cols
            if half == 0 and start >= WHOLE:
                into, place = 1, slice(SIZE[1] + start - WHOLE, SIZE[1] + cols.stop - WHOLE)
            squares = lax.dot_general(
                jnp.ones((8, 128), BF), ssq[half][cols, :].astype(BF), NT, preferred_element_type=F32
            )
            inv = lax.rsqrt(squares[0:1] * (1.0 / 4096.0) + 1e-05)
            gate = acc[half][0:hidden, cols] * inv
            up = acc[half][hid_pad:hid_pad + hidden, cols] * inv
            back = acc_back[half][:, cols]
            sig = jax.nn.sigmoid(gate)
            active = gate * sig
            hid[into][:, place] = (active * up).astype(BF)
            back = back * inv
            dgu[into][0:hidden, place] = (back * up * sig * (1.0 + gate * (1.0 - sig))).astype(BF)
            dgu[into][hid_pad:hid_pad + hidden, place] = (back * active).astype(BF)

    def contracted(half, parts, n):
        if half == 0:
            pair = [parts[0][2 * n + i, 0:WHOLE, :] for i in range(2)]
        else:
            pair = [
                jnp.concatenate([parts[1][2 * n + i], parts[0][2 * n + i, WHOLE:WHOLE + LEFT, :]], axis=0)
                for i in range(2)
            ]
        return jnp.concatenate(pair, axis=1)

    def gradients(half, chunk):
        @pl.loop(0, 4, unroll=2)
        def _(i):
            n = chunk * 4 + i
            cols = pl.ds(pl.multiple_of(n * 256, 256), 256)
            both = jnp.dot(dgu[half][...], contracted(half, rows_in, n), preferred_element_type=F32)
            down = jnp.dot(hid[half][...], contracted(half, rows_cot, n), preferred_element_type=F32)
            if half == 0:
                part_gu[:, cols] = both
                part_d[:, cols] = down
            else:
                both = (both + part_gu[:, cols]).astype(BF)
                stage[0, :, cols] = both[0:hidden]
                stage[1, :, cols] = both[hid_pad:hid_pad + hidden]
                stage[2, :, cols] = (down + part_d[:, cols]).astype(BF)

    run(cot_far, 3)
    run(cot_near, 2)
    run(cot_far)
    run(cot_near, 2)
    run(cot_far)
    exchanged(rows_in, tx_send, tx_recv, 0)
    run(in_near)
    run(cot_own, 4)
    run(cot_far, 3)
    own_back(0, 0, -1, 1, 2)
    run(in_near)
    run(cot_far)
    exchange(route_x, rows_in, tx_send, tx_recv, 1)
    sibling_back(0, 0, -1)
    run(in_near)
    sibling_back(0, 1, 2)
    run(in_near, 3)
    exchanged(rows_in, tx_send, tx_recv, 1)
    run(in_far)
    own_back(1, 0, -1, 1, 2)
    run(in_near)
    sibling_back(1, 0, -1, 1, 2)
    run(in_near)
    own_fore(0, 0)
    run(in_near)
    own_fore(0, -1)
    run(in_far)
    run(in_near)
    own_fore(0, 1)
    run(in_near)
    run(in_far)
    own_fore(0, 2)
    run(in_far)
    sibling_fore(0, 0)
    run(in_far)
    sibling_fore(0, -1)
    run(in_far, 2)
    sibling_fore(0, 1)
    sibling_fore(0, 2)
    run(in_far, 2)
    activations(0)
    gradients(0, 0)
    run(in_far)
    gradients(0, 1)
    run(in_far)
    gradients(0, 2)
    gradients(0, 3)
    own_fore(1, 0, -1, 1, 2)
    sibling_fore(1, 0, -1, 1, 2)
    activations(1)
    outs = (og_ref, ou_ref, od_ref)
    writes = []
    for quarter in range(4):
        gradients(1, quarter)
        cols = pl.ds(quarter * 1024, 1024)
        for index in range(3):
            write = pltpu.make_async_copy(
                stage.at[index, :, cols], outs[index].at[:, cols], out_sem.at[index, quarter]
            )
            write.start()
            writes.append(write)

    assert not any([ctx_steps] + cot_steps + in_steps)
    for gather in (ctx_gather,) + cot_gather + in_gather:
        gather.finish()
    for descriptor in pending:
        descriptor.wait_send()
    for write in writes:
        write.wait()


def write_kernel(*refs):
    count = 3
    sources, outs, hold, sem_in, sem_out = refs[:count], refs[count:2 * count], *refs[2 * count:]
    reads, writes = [], []
    for index in range(count):
        for part in range(4):
            cols = pl.ds(part * 1024, 1024)
            there = hold.at[index, :, cols]
            reads.append(pltpu.make_async_copy(sources[index].at[:, cols], there, sem_in.at[index, part]))
            writes.append(pltpu.make_async_copy(there, outs[index].at[:, cols], sem_out.at[index, part]))
    for read in reads:
        read.start()
    for read, write in zip(reads, writes):
        read.wait()
        write.start()
    for write in writes:
        write.wait()


def per_device(
    context, residual, attn_weight, norm_gain, gate_weight, up_weight, down_weight,
    cotangent, expert_ids, gate_fixed,
):
    hidden = gate_weight.shape[2]
    pad = 176
    dma = pltpu.SemaphoreType.DMA
    vmem = pl.BlockSpec(memory_space=pltpu.VMEM)
    hbm = pl.BlockSpec(memory_space=pl.ANY)
    out = jax.ShapeDtypeStruct((hidden, 4096), BF)
    copies = PlaneGather.COPIES
    near, far = SIZE
    grads = pl.pallas_call(
        kernel,
        out_shape=(out, out, out),
        in_specs=[hbm, hbm, hbm, hbm, vmem, vmem, vmem, hbm, hbm, hbm],
        out_specs=(hbm, hbm, hbm),
        scratch_shapes=[
            pltpu.VMEM((32, near, 128), BF),
            pltpu.VMEM((32, far, 128), BF),
            pltpu.VMEM((32, near, 128), BF),
            pltpu.VMEM((32, far, 128), BF),
            pltpu.VMEM((32, 128, 512), BF),
            pltpu.VMEM((2 * pad, 4096), BF),
            pltpu.VMEM((hidden, 4096), BF),
            pltpu.VMEM((2, hidden, 4096), BF),
            pltpu.VMEM((2 * pad, near), F32),
            pltpu.VMEM((2 * pad, far), F32),
            pltpu.VMEM((hidden, near), F32),
            pltpu.VMEM((hidden, far), F32),
            pltpu.VMEM((near, 128), F32),
            pltpu.VMEM((far, 128), F32),
            pltpu.VMEM((2 * pad, WHOLE), BF),
            pltpu.VMEM((2 * pad, far + LEFT), BF),
            pltpu.VMEM((hidden, WHOLE), BF),
            pltpu.VMEM((hidden, far + LEFT), BF),
            pltpu.VMEM((2 * pad, 4096), F32),
            pltpu.VMEM((hidden, 4096), F32),
            pltpu.VMEM((3, hidden, 4096), BF),
            pltpu.VMEM((32, 128), F32),
            pltpu.VMEM((512, 1024), BF),
            pltpu.VMEM((4, PARTS, 64, 1024 // PARTS), BF),
            pltpu.VMEM((3, PARTS, 64, 1024 // PARTS), BF),
            pltpu.VMEM((3, PARTS, 64, 1024 // PARTS), BF),
            pltpu.VMEM((2, PARTS, 64, 1024 // PARTS), BF),
            pltpu.VMEM((8, 64, 128), BF),
            pltpu.VMEM((8, 512, 128), BF),
            pltpu.VMEM((512, 128), F32),
            pltpu.VMEM((512, 128), BF),
            pltpu.VMEM((512, 128), BF),
            pltpu.VMEM((4, 8, 128), F32),
            pltpu.VMEM((1280, 512), BF),
            pltpu.VMEM((8, 160, 128), BF),
            pltpu.VMEM((8, 160, 128), BF),
            dma((3,)),
            dma((copies,)), dma((copies,)), dma((copies,)), dma((copies,)),
            dma((copies,)), dma((copies,)), dma((copies,)), dma((copies,)),
            dma((copies,)), dma((copies,)),
            dma((copies,)), dma((copies,)), dma((2,)),
            dma((3, 4)), dma((3, 4)), dma((2,)),
            dma((4, PARTS)), dma((4, PARTS)), dma((3, PARTS)), dma((3, PARTS)),
            dma((8,)), dma((8,)),
            dma((2, 4, PARTS)), dma((2, 4, PARTS)),
            dma((8,)), dma((8,)),
            dma((8,)), dma((8,)),
            dma((3, 4)),
        ],
        compiler_params=pltpu.CompilerParams(
            collective_id=0, has_side_effects=True, vmem_limit_bytes=67_000_000
        ),
    )(
        attn_weight[0], context, residual, cotangent, expert_ids.T, gate_fixed.T, norm_gain,
        gate_weight[0].T, up_weight[0].T, down_weight[0],
    )
    grads = pl.pallas_call(
        write_kernel,
        out_shape=(out, out, out),
        in_specs=[hbm, hbm, hbm],
        out_specs=(hbm, hbm, hbm),
        scratch_shapes=[pltpu.VMEM((3, hidden, 4096), BF), dma((3, 4)), dma((3, 4))],
    )(*grads)
    return grads[0].T[None], grads[1].T[None], grads[2][None]


def solution(mesh):
    return jax.shard_map(
        per_device,
        mesh=mesh,
        in_specs=(
            P(("branch", "dp"), "mp"),
            P(("branch", "dp"), None),
            P("branch", "mp", "dp"),
            P(),
            P("branch", None, ("mp", "dp")),
            P("branch", None, ("mp", "dp")),
            P("branch", ("mp", "dp"), None),
            P(("branch", "dp"), None),
            P(("branch", "dp"), None),
            P(("branch", "dp"), None),
        ),
        out_specs=(
            P("branch", None, ("mp", "dp")),
            P("branch", None, ("mp", "dp")),
            P("branch", ("mp", "dp"), None),
        ),
        check_vma=False,
    )
```

```python
import functools

import jax
import jax.numpy as jnp
from jax import lax
from jax.experimental import pallas as pl
from jax.experimental.pallas import tpu as pltpu
from jax.sharding import PartitionSpec as P

MESH = pl.DeviceIdType.MESH
BF = jnp.bfloat16
F32 = jnp.float32
NT = (((1,), (1,)), ((), ()))


class Coords:
    def __init__(self):
        self.z = lax.axis_index("branch")
        self.mp = lax.axis_index("mp")
        self.dp = lax.axis_index("dp")
        self.x = lax.rem(self.mp, 4)
        self.core = lax.rem(self.dp, 2)
        self.y = lax.div(self.dp, 2) * 2 + lax.div(self.mp, 4)

    def at(self, da, db, core):
        other = 1 - core
        x = lax.rem(self.x + other * da + core * db + 8, 4)
        y = lax.rem(self.y + core * da + other * db + 8, 4)
        return x, y

    def device(self, da, db):
        x, y = self.at(da, db, self.core)
        return (self.z, lax.rem(y, 2) * 4 + x, lax.div(y, 2) * 2 + self.core)

    def piece(self, da, db, core=None):
        core = self.core if core is None else core
        x, y = self.at(da, db, core)
        return (lax.div(y, 2) * 2 + core) * 8 + lax.rem(y, 2) * 4 + x

    def sibling(self):
        return (self.z, self.mp, self.dp + 1 - 2 * self.core)


RING = (0, -1, 1, 2)


class PlaneGather:
    COPIES = 36

    def __init__(self, at, buf, send, recv, start=0, size=None):
        self.at, self.buf, self.send, self.recv = at, buf, send, recv
        self.base, self.size = start, buf.shape[1] if size is None else size
        self.half = self.size // 2
        self.sent = []

    def view(self, piece, half=None):
        if half is None:
            return self.buf.at[piece, pl.ds(self.base, self.size)]
        return self.buf.at[piece, pl.ds(self.base + half * self.half, self.half)]

    def copy(self, index, piece, device, half=None):
        ref = self.view(piece, half)
        return pltpu.make_async_remote_copy(
            src_ref=ref,
            dst_ref=ref,
            send_sem=self.send.at[index],
            recv_sem=self.recv.at[index],
            device_id=device,
            device_id_type=MESH,
        )

    def go(self, index, piece, device, half=None):
        descriptor = self.copy(index, piece, device, half)
        descriptor.start()
        self.sent.append(descriptor)

    def arrived(self, index, piece, half=None):
        self.copy(index, piece, self.at.sibling(), half).wait_recv()

    def to_sibling(self, qa, qb):
        index = 20 + 4 * RING.index(qa) + RING.index(qb)
        self.go(index, self.at.piece(qa, qb), self.at.sibling())

    def spread(self, qa):
        index = 4 + 4 * RING.index(qa)
        piece = self.at.piece(qa, 0)
        self.go(index, piece, self.at.device(0, 1))
        self.go(index + 1, piece, self.at.device(0, -1))
        self.to_sibling(qa, 0)

    def start(self):
        piece = self.at.piece(0, 0)
        self.go(0, piece, self.at.device(1, 0))
        self.go(1, piece, self.at.device(-1, 0))
        self.spread(0)

    def first_axis(self):
        low, high = self.at.piece(-1, 0), self.at.piece(1, 0)
        self.arrived(0, low)
        self.go(2, low, self.at.device(1, 0), 0)
        self.arrived(1, high)
        self.go(3, high, self.at.device(-1, 0), 1)
        self.spread(-1)
        self.spread(1)

    def first_axis_far(self):
        far = self.at.piece(2, 0)
        self.arrived(2, far, 0)
        self.arrived(3, far, 1)
        self.spread(2)

    def relay(self, qa):
        index = 4 + 4 * RING.index(qa)
        low, high = self.at.piece(qa, -1), self.at.piece(qa, 1)
        self.arrived(index, low)
        self.go(index + 2, low, self.at.device(0, 1), 0)
        self.arrived(index + 1, high)
        self.go(index + 3, high, self.at.device(0, -1), 1)
        self.to_sibling(qa, -1)
        self.to_sibling(qa, 1)

    def far(self, qa):
        index = 4 + 4 * RING.index(qa)
        piece = self.at.piece(qa, 2)
        self.arrived(index + 2, piece, 0)
        self.arrived(index + 3, piece, 1)
        self.to_sibling(qa, 2)

    def from_sibling(self, qa):
        for qb in RING:
            index = 20 + 4 * RING.index(qa) + RING.index(qb)
            self.arrived(index, self.at.piece(qa, qb, 1 - self.at.core))

    def own_group(self, qa):
        return [self.at.piece(qa, qb) for qb in RING]

    def sibling_group(self, qa):
        return [self.at.piece(qa, qb, 1 - self.at.core) for qb in RING]

    def steps(self):
        return [
            self.start,
            self.first_axis,
            self.first_axis_far,
            functools.partial(self.relay, 0),
            functools.partial(self.relay, -1),
            functools.partial(self.relay, 1),
            functools.partial(self.relay, 2),
            functools.partial(self.far, 0),
            functools.partial(self.far, -1),
            functools.partial(self.far, 1),
            functools.partial(self.far, 2),
        ]

    def finish(self):
        for descriptor in self.sent:
            descriptor.wait_send()


POSITION = {0: 0, 1: 1, 7: 2, 2: 3, 6: 4, 3: 5, 5: 6, 4: 7}
NEAR = 5
SIZE = (NEAR * 160, (8 - NEAR) * 160)
WHOLE = SIZE[0] // 256 * 256
LEFT = SIZE[0] - WHOLE
PARTS = 4
CAP = 40


def kernel(
    attn_hbm, context_ref, residual_ref, cot_ref, ids_ref, gates_ref, gain1_ref, wg_ref, wu_ref, wd_ref,
    og_ref, ou_ref, od_ref,
    rows_in0, rows_in1, rows_cot0, rows_cot1, ctx_all, wgu, wd, wtmp, acc0, acc1, back0, back1, ssq0, ssq1, dgu0, dgu1, hid0, hid1,
    part_gu, part_d, stage, gain_ref, attn_ref,
    red_in_l, red_in_s, red_out_l, red_out_s, red_sum, merged_all, attn_acc,
    res_all, cot_all, info_all, sel, route_x, route_c,
    w_sem, in0_send, in0_recv, in1_send, in1_recv,
    cotz_send, cotz_recv, cot0_send, cot0_recv, cot1_send, cot1_recv,
    ctx_send, ctx_recv, in_local, ex_send, ex_recv, ex_local,
    rl_send, rl_recv, rs_send, rs_recv, ma_send, ma_recv, ga_send, ga_recv,
    tx_send, tx_recv, tc_send, tc_recv, out_sem,
):
    at = Coords()
    z, mp, dp = at.z, at.mp, at.dp
    own = at.piece(0, 0)
    hidden = wg_ref.shape[0]
    hid_pad = wgu.shape[0] // 2
    rows_in = (rows_in0, rows_in1)
    acc, acc_back, ssq, dgu, hid = (acc0, acc1), (back0, back1), (ssq0, ssq1), (dgu0, dgu1), (hid0, hid1)
    rows_cot = (rows_cot0, rows_cot1)
    pending = []

    def z_dev(k):
        return (lax.rem(z + k + 8, 8), mp, dp)

    def mp_dev(k):
        return (z, lax.rem(mp + k, 8), dp)

    def dp_dev(k):
        return (z, mp, lax.rem(dp + k, 4))

    def remote(src, dst, send, recv, device):
        return pltpu.make_async_remote_copy(
            src_ref=src, dst_ref=dst, send_sem=send, recv_sem=recv,
            device_id=device, device_id_type=MESH,
        )

    def push(src, dst, send, recv, device):
        descriptor = remote(src, dst, send, recv, device)
        descriptor.start()
        pending.append(descriptor)

    def landed(dst, recv, send):
        remote(dst, dst, send, recv, at.sibling()).wait_recv()

    barrier = pltpu.get_barrier_semaphore()
    peers = [z_dev(k) for k in range(1, 8)] + [mp_dev(k) for k in range(1, 8)]
    peers += [dp_dev(k) for k in range(1, 4)]
    for dy in (1, -1):
        y = lax.rem(at.y + dy + 4, 4)
        peers.append((z, lax.rem(y, 2) * 4 + at.x, lax.div(y, 2) * 2 + at.core))
    for peer in peers:
        pl.semaphore_signal(barrier, inc=1, device_id=peer, device_id_type=MESH)

    ctx_copy = pltpu.make_async_copy(context_ref, ctx_all.at[own], in_local.at[0])
    ctx_copy.start()
    dp_rows = pl.ds(pl.multiple_of(dp * 128, 128), 128)

    def columns(k):
        d = lax.rem(dp + k, 4)
        return pl.ds(pl.multiple_of(d * 1024 + mp * 128, 128), 128)

    locals_ = [
        pltpu.make_async_copy(residual_ref.at[:, columns(0)], res_all.at[dp_rows], ex_local.at[0]),
        pltpu.make_async_copy(cot_ref.at[:, columns(0)], cot_all.at[dp_rows], ex_local.at[1]),
    ]
    attn_copy = pltpu.make_async_copy(attn_hbm, attn_ref, in_local.at[1])
    attn_copy.start()
    for copy in locals_:
        copy.start()

    gain_ref[...] = gain1_ref[...].astype(F32).reshape(32, 128)

    ids = ids_ref[...]
    experts = lax.broadcasted_iota(jnp.int32, (8, 128), 0)
    first = jnp.where(experts == ids[0:1, :], 1.0, 0.0)
    second = jnp.where(experts == ids[1:2, :], 1.0, 0.0)
    before = jnp.where(
        lax.broadcasted_iota(jnp.int32, (128, 128), 0) < lax.broadcasted_iota(jnp.int32, (128, 128), 1),
        1.0, 0.0,
    ).astype(BF)
    counts = jnp.dot(
        jnp.concatenate([first, second], axis=0).astype(BF), before, preferred_element_type=F32
    )
    slot0 = jnp.sum(first * counts[0:8], axis=0, keepdims=True)
    slot1 = jnp.sum(
        second * (counts[8:16] + jnp.sum(first, axis=1, keepdims=True)), axis=0, keepdims=True
    )
    base = (ids * 160 + dp * CAP).astype(F32)
    code0 = jnp.where(slot0 < CAP, base[0:1] + slot0, -1.0)
    code1 = jnp.where(slot1 < CAP, base[1:2] + slot1, -1.0)
    gates = gates_ref[...].astype(F32) / 32768.0
    info_all[dp] = jnp.concatenate([code0, code1, gates, jnp.zeros((4, 128), F32)], axis=0)
    pl.semaphore_wait(barrier, len(peers))

    for k in range(1, 4):
        push(cot_ref.at[:, columns(k)], cot_all.at[dp_rows], ex_send.at[0, k], ex_recv.at[0, k], dp_dev(k))
        push(info_all.at[dp], info_all.at[dp], ex_send.at[1, k], ex_recv.at[1, k], dp_dev(k))

    def chunk(k):
        t = lax.rem(z + k + 8, 8)
        return pl.ds(pl.multiple_of(t * 64, 64), 64)

    width = 1024 // PARTS
    part_cols = [pl.ds(h * width, width) for h in range(PARTS)]

    def reduce_step(step):
        for h in range(PARTS):
            cols = part_cols[h]
            sign = 1 - 2 * (h % 2)
            if step < 4:
                part = chunk(sign * (4 - step))
                src = attn_hbm.at[part, cols]
                if step > 0:
                    landed(red_in_l.at[step - 1, h], rl_recv.at[step - 1, h], rl_send.at[step - 1, h])
                    red_out_l[step - 1, h] = (
                        red_in_l[step - 1, h].astype(F32) + attn_ref[part, cols].astype(F32)
                    ).astype(BF)
                    src = red_out_l.at[step - 1, h]
                push(src, red_in_l.at[step, h], rl_send.at[step, h], rl_recv.at[step, h], z_dev(sign))
            if step < 3:
                part = chunk(-sign * (3 - step))
                src = attn_hbm.at[part, cols]
                if step > 0:
                    landed(red_in_s.at[step - 1, h], rs_recv.at[step - 1, h], rs_send.at[step - 1, h])
                    red_out_s[step - 1, h] = (
                        red_in_s[step - 1, h].astype(F32) + attn_ref[part, cols].astype(F32)
                    ).astype(BF)
                    src = red_out_s.at[step - 1, h]
                push(src, red_in_s.at[step, h], rs_send.at[step, h], rs_recv.at[step, h], z_dev(-sign))

    reduce_step(0)

    ctx_gather = PlaneGather(at, ctx_all, ctx_send, ctx_recv)
    rest = SIZE[0] - 160
    cot_gather = (
        PlaneGather(at, rows_cot0, cot0_send, cot0_recv, 160, rest),
        PlaneGather(at, rows_cot1, cot1_send, cot1_recv),
        PlaneGather(at, rows_cot0, cotz_send, cotz_recv, 0, 160),
    )
    in_gather = (
        PlaneGather(at, rows_in0, in0_send, in0_recv),
        PlaneGather(at, rows_in1, in1_send, in1_recv),
    )
    ctx_steps = ctx_gather.steps()
    cot_steps = [gather.steps() for gather in cot_gather]
    in_steps = [gather.steps() for gather in in_gather]

    def run(steps, count=1):
        for _ in range(count):
            if steps:
                steps.pop(0)()

    ctx_copy.wait()
    run(ctx_steps)

    weights = [
        pltpu.make_async_copy(wg_ref, wtmp.at[0], w_sem.at[0]),
        pltpu.make_async_copy(wu_ref, wtmp.at[1], w_sem.at[1]),
        pltpu.make_async_copy(wd_ref, wd, w_sem.at[2]),
    ]
    for copy in weights:
        copy.start()

    def from_group(k):
        d = lax.rem(dp - k + 4, 4)
        return pl.ds(pl.multiple_of(d * 128, 128), 128), d

    attn_copy.wait()
    reduce_step(1)
    locals_[1].wait()
    for k in range(1, 4):
        rows, d = from_group(k)
        landed(cot_all.at[rows], ex_recv.at[0, k], ex_send.at[0, k])
        landed(info_all.at[d], ex_recv.at[1, k], ex_send.at[1, k])

    @pl.loop(0, 8, unroll=2)
    def _(e):
        place = (lax.broadcasted_iota(jnp.int32, (160, 128), 0) + e * 160).astype(F32)
        row_gate = jnp.zeros((160, 1), F32)
        rows = pl.ds(pl.multiple_of(e * 160, 160), 160)
        for d in range(4):
            info = info_all[d]
            first = place == info[0:1, :]
            second = place == info[1:2, :]
            sel[rows, d * 128:(d + 1) * 128] = jnp.where(first | second, 1.0, 0.0).astype(BF)
            gates = jnp.where(first, info[2:3, :], jnp.where(second, info[3:4, :], 0.0))
            row_gate += jnp.sum(gates, axis=1, keepdims=True)
        picked = jnp.dot(sel[rows, :], cot_all[...], preferred_element_type=F32)
        route_c[e] = (picked * row_gate).astype(BF)

    def block(k):
        place = POSITION[k]
        if place < NEAR:
            return 0, pl.ds(place * 160, 160)
        return 1, pl.ds((place - NEAR) * 160, 160)

    def exchange(route, gathered, send, recv, wanted):
        if wanted == 0:
            half, rows = block(0)
            gathered[half][own, rows, :] = route[z]
        for k in sorted(range(1, 8), key=lambda k: POSITION[k]):
            half, rows = block(k)
            e = lax.rem(z - k + 8, 8)
            if half == wanted:
                push(route.at[e], gathered[half].at[own, rows], send.at[k], recv.at[k], z_dev(-k))

    def exchanged(gathered, send, recv, wanted):
        for k in range(1, 8):
            half, rows = block(k)
            if half == wanted:
                landed(gathered[half].at[own, rows], recv.at[k], send.at[k])

    cot_near, cot_far, cot_own = cot_steps
    in_near, in_far = in_steps
    run(ctx_steps)
    reduce_step(2)
    exchange(route_c, rows_cot, tc_send, tc_recv, 0)
    run(cot_own)
    for k in range(1, 4):
        push(residual_ref.at[:, columns(k)], res_all.at[dp_rows], ex_send.at[2, k], ex_recv.at[2, k], dp_dev(k))
    run(ctx_steps, 2)
    reduce_step(3)
    run(cot_own)
    run(ctx_steps, 2)

    for h in range(PARTS):
        landed(red_in_l.at[3, h], rl_recv.at[3, h], rl_send.at[3, h])
        landed(red_in_s.at[2, h], rs_recv.at[2, h], rs_send.at[2, h])
        total = (
            red_in_l[3, h].astype(F32) + red_in_s[2, h].astype(F32)
            + attn_ref[chunk(0), part_cols[h]].astype(F32)
        )
        mean = (total * 0.125).astype(BF)
        for part in range(8 // PARTS):
            red_sum[8 // PARTS * h + part] = mean[:, part * 128:(part + 1) * 128]
    own_rows = pl.ds(pl.multiple_of(z * 64, 64), 64)
    for k in range(1, 8):
        j = lax.rem(mp + k, 8)
        push(red_sum.at[j], merged_all.at[mp, own_rows], ma_send.at[k], ma_recv.at[k], mp_dev(k))
    merged_all[mp, own_rows, :] = red_sum[mp]
    exchange(route_c, rows_cot, tc_send, tc_recv, 1)
    exchanged(rows_cot, tc_send, tc_recv, 0)
    run(cot_near)
    run(ctx_steps)
    run(cot_own, 2)
    for k in range(1, 8):
        j = lax.rem(mp - k + 8, 8)
        landed(merged_all.at[j, own_rows], ma_recv.at[k], ma_send.at[k])

    def merged_view(k, h):
        t = lax.rem(z + k + 8, 8)
        return merged_all.at[pl.ds(8 // PARTS * h, 8 // PARTS), pl.ds(pl.multiple_of(t * 64, 64), 64)]

    def gather_step(step):
        for h in range(PARTS):
            sign = 1 - 2 * (h % 2)
            if step > 0:
                landed(merged_view(-sign * step, h), ga_recv.at[0, step - 1, h], ga_send.at[0, step - 1, h])
            if step < 4:
                view = merged_view(-sign * step, h)
                push(view, view, ga_send.at[0, step, h], ga_recv.at[0, step, h], z_dev(sign))
            if 0 < step < 4:
                landed(merged_view(sign * step, h), ga_recv.at[1, step - 1, h], ga_send.at[1, step - 1, h])
            if step < 3:
                view = merged_view(sign * step, h)
                push(view, view, ga_send.at[1, step, h], ga_recv.at[1, step, h], z_dev(-sign))

    gather_step(0)
    run(ctx_steps, 2)
    run(cot_own, 2)
    run(cot_near)
    gather_step(1)
    run(cot_near, 2)
    exchanged(rows_cot, tc_send, tc_recv, 1)
    run(cot_far)
    run(ctx_steps, 2)
    gather_step(2)
    run(cot_near, 2)
    run(cot_own)
    gather_step(3)
    run(cot_far)
    run(cot_near)
    for qa in RING:
        ctx_gather.from_sibling(qa)
    for k in range(1, 4):
        rows, _ = from_group(k)
        landed(res_all.at[rows], ex_recv.at[2, k], ex_send.at[2, k])
    locals_[0].wait()

    last = lax.div(lax.rem(z + 4, 8), 2)

    def feature_product(terms):
        context = jnp.concatenate(
            [
                jnp.concatenate([ctx_all[d * 8 + j, :, pairs] for j, pairs in terms], axis=1)
                for d in range(4)
            ],
            axis=0,
        )
        weight = jnp.concatenate([merged_all[j, pairs, :] for j, pairs in terms], axis=0)
        return jnp.dot(context, weight, preferred_element_type=F32)

    def pair_of(k):
        return pl.ds(pl.multiple_of(lax.rem(last + k, 4) * 128, 128), 128)

    attn_acc[...] = res_all[...].astype(F32)
    for j in range(0, 8, 2):
        attn_acc[...] += feature_product([(j + i, pair_of(k)) for i in range(2) for k in range(1, 4)])
    gather_step(4)

    def lanes(piece):
        return pl.ds(pl.multiple_of(piece * 128, 128), 128)

    def gain_of(piece):
        return gain_ref[pl.ds(piece, 1), :]

    attn_acc[...] += feature_product([(j, pair_of(0)) for j in range(8)])
    res_all[...] = (attn_acc[...] * gain_of(own)).astype(BF)

    picked = jnp.dot(sel[...], res_all[...], preferred_element_type=F32).astype(BF)
    route_x[...] = picked.reshape(8, 160, 128)

    exchange(route_x, rows_in, tx_send, tx_recv, 0)

    for copy in weights:
        copy.wait()
    wgu[0:hidden, :] = wtmp[0]
    wgu[hid_pad:hid_pad + hidden, :] = wtmp[1]
    for ref in acc + acc_back + ssq:
        ref[...] = jnp.zeros_like(ref)

    def tiles(half):
        return [(start, min(256, SIZE[half] - start)) for start in range(0, SIZE[half], 256)]

    def back_group(half, group):
        lhs = jnp.concatenate([wd[:, lanes(p)] for p in group], axis=1)
        for start, width in tiles(half):
            rhs = jnp.concatenate([rows_cot[half][p, start:start + width, :] for p in group], axis=1)
            cols = slice(start, start + width)
            acc_back[half][:, cols] += lax.dot_general(lhs, rhs, NT, preferred_element_type=F32)

    def fore_group(half, group):
        lhs = jnp.concatenate([wgu[:, lanes(p)] for p in group], axis=1)
        inverse = [1.0 / gain_of(p) for p in group]
        for start, width in tiles(half):
            parts = [rows_in[half][p, start:start + width, :] for p in group]
            cols = slice(start, start + width)
            acc[half][:, cols] += lax.dot_general(
                lhs, jnp.concatenate(parts, axis=1), NT, preferred_element_type=F32
            )
            squares = ssq[half][cols, :]
            for part, scale in zip(parts, inverse):
                value = part.astype(F32) * scale
                squares += value * value
            ssq[half][cols, :] = squares

    def own_back(half, *places):
        for qa in places:
            back_group(half, cot_gather[half].own_group(qa))

    def sibling_back(half, *places):
        for qa in places:
            if half == 0:
                cot_gather[2].from_sibling(qa)
            cot_gather[half].from_sibling(qa)
            back_group(half, cot_gather[half].sibling_group(qa))

    def own_fore(half, *places):
        for qa in places:
            fore_group(half, in_gather[half].own_group(qa))

    def sibling_fore(half, *places):
        for qa in places:
            in_gather[half].from_sibling(qa)
            fore_group(half, in_gather[half].sibling_group(qa))

    def activations(half):
        for start in range(0, SIZE[half], 128):
            cols = slice(start, min(start + 128, SIZE[half]))
            into, place = half, cols
            if half == 0 and start >= WHOLE:
                into, place = 1, slice(SIZE[1] + start - WHOLE, SIZE[1] + cols.stop - WHOLE)
            squares = lax.dot_general(
                jnp.ones((8, 128), BF), ssq[half][cols, :].astype(BF), NT, preferred_element_type=F32
            )
            inv = lax.rsqrt(squares[0:1] * (1.0 / 4096.0) + 1e-05)
            gate = acc[half][0:hidden, cols] * inv
            up = acc[half][hid_pad:hid_pad + hidden, cols] * inv
            back = acc_back[half][:, cols]
            sig = jax.nn.sigmoid(gate)
            active = gate * sig
            hid[into][:, place] = (active * up).astype(BF)
            back = back * inv
            dgu[into][0:hidden, place] = (back * up * sig * (1.0 + gate * (1.0 - sig))).astype(BF)
            dgu[into][hid_pad:hid_pad + hidden, place] = (back * active).astype(BF)

    def contracted(half, parts, n):
        if half == 0:
            pair = [parts[0][2 * n + i, 0:WHOLE, :] for i in range(2)]
        else:
            pair = [
                jnp.concatenate([parts[1][2 * n + i], parts[0][2 * n + i, WHOLE:WHOLE + LEFT, :]], axis=0)
                for i in range(2)
            ]
        return jnp.concatenate(pair, axis=1)

    def gradients(half, chunk):
        @pl.loop(0, 4, unroll=2)
        def _(i):
            n = chunk * 4 + i
            cols = pl.ds(pl.multiple_of(n * 256, 256), 256)
            both = jnp.dot(dgu[half][...], contracted(half, rows_in, n), preferred_element_type=F32)
            down = jnp.dot(hid[half][...], contracted(half, rows_cot, n), preferred_element_type=F32)
            if half == 0:
                part_gu[:, cols] = both
                part_d[:, cols] = down
            else:
                both = (both + part_gu[:, cols]).astype(BF)
                stage[0, :, cols] = both[0:hidden]
                stage[1, :, cols] = both[hid_pad:hid_pad + hidden]
                stage[2, :, cols] = (down + part_d[:, cols]).astype(BF)

    run(cot_far, 3)
    run(cot_near, 2)
    run(cot_far)
    run(cot_near, 2)
    exchanged(rows_in, tx_send, tx_recv, 0)
    run(in_near)
    run(cot_far)
    run(cot_own, 4)
    run(cot_far, 3)
    own_back(0, 0, -1, 1, 2)
    run(in_near)
    run(cot_far)
    exchange(route_x, rows_in, tx_send, tx_recv, 1)
    sibling_back(0, 0, -1)
    run(in_near)
    sibling_back(0, 1, 2)
    run(in_near, 3)
    exchanged(rows_in, tx_send, tx_recv, 1)
    run(in_far)
    own_back(1, 0, -1, 1, 2)
    run(in_near)
    sibling_back(1, 0, -1, 1, 2)
    run(in_near)
    own_fore(0, 0)
    run(in_near)
    own_fore(0, -1)
    run(in_far)
    run(in_near)
    own_fore(0, 1)
    run(in_near)
    run(in_far)
    own_fore(0, 2)
    run(in_far)
    sibling_fore(0, 0)
    run(in_far)
    sibling_fore(0, -1)
    run(in_far)
    sibling_fore(0, 1)
    sibling_fore(0, 2)
    activations(0)
    run(in_far)
    gradients(0, 0)
    run(in_far, 2)
    gradients(0, 1)
    run(in_far, 2)
    gradients(0, 2)
    gradients(0, 3)
    own_fore(1, 0, -1, 1, 2)
    sibling_fore(1, 0, -1, 1, 2)
    activations(1)
    outs = (og_ref, ou_ref, od_ref)
    writes = []
    for quarter in range(4):
        gradients(1, quarter)
        cols = pl.ds(quarter * 1024, 1024)
        for index in range(3):
            write = pltpu.make_async_copy(
                stage.at[index, :, cols], outs[index].at[:, cols], out_sem.at[index, quarter]
            )
            write.start()
            writes.append(write)

    assert not any([ctx_steps] + cot_steps + in_steps)
    for gather in (ctx_gather,) + cot_gather + in_gather:
        gather.finish()
    for descriptor in pending:
        descriptor.wait_send()
    for write in writes:
        write.wait()


def write_kernel(*refs):
    count = 3
    sources, outs, hold, sem_in, sem_out = refs[:count], refs[count:2 * count], *refs[2 * count:]
    reads, writes = [], []
    for index in range(count):
        for part in range(4):
            cols = pl.ds(part * 1024, 1024)
            there = hold.at[index, :, cols]
            reads.append(pltpu.make_async_copy(sources[index].at[:, cols], there, sem_in.at[index, part]))
            writes.append(pltpu.make_async_copy(there, outs[index].at[:, cols], sem_out.at[index, part]))
    for read in reads:
        read.start()
    for read, write in zip(reads, writes):
        read.wait()
        write.start()
    for write in writes:
        write.wait()


def per_device(
    context, residual, attn_weight, norm_gain, gate_weight, up_weight, down_weight,
    cotangent, expert_ids, gate_fixed,
):
    hidden = gate_weight.shape[2]
    pad = 176
    dma = pltpu.SemaphoreType.DMA
    vmem = pl.BlockSpec(memory_space=pltpu.VMEM)
    hbm = pl.BlockSpec(memory_space=pl.ANY)
    out = jax.ShapeDtypeStruct((hidden, 4096), BF)
    copies = PlaneGather.COPIES
    near, far = SIZE
    grads = pl.pallas_call(
        kernel,
        out_shape=(out, out, out),
        in_specs=[hbm, hbm, hbm, hbm, vmem, vmem, vmem, hbm, hbm, hbm],
        out_specs=(hbm, hbm, hbm),
        scratch_shapes=[
            pltpu.VMEM((32, near, 128), BF),
            pltpu.VMEM((32, far, 128), BF),
            pltpu.VMEM((32, near, 128), BF),
            pltpu.VMEM((32, far, 128), BF),
            pltpu.VMEM((32, 128, 512), BF),
            pltpu.VMEM((2 * pad, 4096), BF),
            pltpu.VMEM((hidden, 4096), BF),
            pltpu.VMEM((2, hidden, 4096), BF),
            pltpu.VMEM((2 * pad, near), F32),
            pltpu.VMEM((2 * pad, far), F32),
            pltpu.VMEM((hidden, near), F32),
            pltpu.VMEM((hidden, far), F32),
            pltpu.VMEM((near, 128), F32),
            pltpu.VMEM((far, 128), F32),
            pltpu.VMEM((2 * pad, WHOLE), BF),
            pltpu.VMEM((2 * pad, far + LEFT), BF),
            pltpu.VMEM((hidden, WHOLE), BF),
            pltpu.VMEM((hidden, far + LEFT), BF),
            pltpu.VMEM((2 * pad, 4096), F32),
            pltpu.VMEM((hidden, 4096), F32),
            pltpu.VMEM((3, hidden, 4096), BF),
            pltpu.VMEM((32, 128), F32),
            pltpu.VMEM((512, 1024), BF),
            pltpu.VMEM((4, PARTS, 64, 1024 // PARTS), BF),
            pltpu.VMEM((3, PARTS, 64, 1024 // PARTS), BF),
            pltpu.VMEM((3, PARTS, 64, 1024 // PARTS), BF),
            pltpu.VMEM((2, PARTS, 64, 1024 // PARTS), BF),
            pltpu.VMEM((8, 64, 128), BF),
            pltpu.VMEM((8, 512, 128), BF),
            pltpu.VMEM((512, 128), F32),
            pltpu.VMEM((512, 128), BF),
            pltpu.VMEM((512, 128), BF),
            pltpu.VMEM((4, 8, 128), F32),
            pltpu.VMEM((1280, 512), BF),
            pltpu.VMEM((8, 160, 128), BF),
            pltpu.VMEM((8, 160, 128), BF),
            dma((3,)),
            dma((copies,)), dma((copies,)), dma((copies,)), dma((copies,)),
            dma((copies,)), dma((copies,)), dma((copies,)), dma((copies,)),
            dma((copies,)), dma((copies,)),
            dma((copies,)), dma((copies,)), dma((2,)),
            dma((3, 4)), dma((3, 4)), dma((2,)),
            dma((4, PARTS)), dma((4, PARTS)), dma((3, PARTS)), dma((3, PARTS)),
            dma((8,)), dma((8,)),
            dma((2, 4, PARTS)), dma((2, 4, PARTS)),
            dma((8,)), dma((8,)),
            dma((8,)), dma((8,)),
            dma((3, 4)),
        ],
        compiler_params=pltpu.CompilerParams(
            collective_id=0, has_side_effects=True, vmem_limit_bytes=67_000_000
        ),
    )(
        attn_weight[0], context, residual, cotangent, expert_ids.T, gate_fixed.T, norm_gain,
        gate_weight[0].T, up_weight[0].T, down_weight[0],
    )
    grads = pl.pallas_call(
        write_kernel,
        out_shape=(out, out, out),
        in_specs=[hbm, hbm, hbm],
        out_specs=(hbm, hbm, hbm),
        scratch_shapes=[pltpu.VMEM((3, hidden, 4096), BF), dma((3, 4)), dma((3, 4))],
    )(*grads)
    return grads[0].T[None], grads[1].T[None], grads[2][None]


def solution(mesh):
    return jax.shard_map(
        per_device,
        mesh=mesh,
        in_specs=(
            P(("branch", "dp"), "mp"),
            P(("branch", "dp"), None),
            P("branch", "mp", "dp"),
            P(),
            P("branch", None, ("mp", "dp")),
            P("branch", None, ("mp", "dp")),
            P("branch", ("mp", "dp"), None),
            P(("branch", "dp"), None),
            P(("branch", "dp"), None),
            P(("branch", "dp"), None),
        ),
        out_specs=(
            P("branch", None, ("mp", "dp")),
            P("branch", None, ("mp", "dp")),
            P("branch", ("mp", "dp"), None),
        ),
        check_vma=False,
    )
```

```python
import functools

import jax
import jax.numpy as jnp
from jax import lax
from jax.experimental import pallas as pl
from jax.experimental.pallas import tpu as pltpu
from jax.sharding import PartitionSpec as P

MESH = pl.DeviceIdType.MESH
BF = jnp.bfloat16
F32 = jnp.float32
NT = (((1,), (1,)), ((), ()))


class Coords:
    def __init__(self):
        self.z = lax.axis_index("branch")
        self.mp = lax.axis_index("mp")
        self.dp = lax.axis_index("dp")
        self.x = lax.rem(self.mp, 4)
        self.core = lax.rem(self.dp, 2)
        self.y = lax.div(self.dp, 2) * 2 + lax.div(self.mp, 4)

    def at(self, da, db, core):
        other = 1 - core
        x = lax.rem(self.x + other * da + core * db + 8, 4)
        y = lax.rem(self.y + core * da + other * db + 8, 4)
        return x, y

    def device(self, da, db):
        x, y = self.at(da, db, self.core)
        return (self.z, lax.rem(y, 2) * 4 + x, lax.div(y, 2) * 2 + self.core)

    def piece(self, da, db, core=None):
        core = self.core if core is None else core
        x, y = self.at(da, db, core)
        return (lax.div(y, 2) * 2 + core) * 8 + lax.rem(y, 2) * 4 + x

    def sibling(self):
        return (self.z, self.mp, self.dp + 1 - 2 * self.core)


RING = (0, -1, 1, 2)


class PlaneGather:
    COPIES = 36

    def __init__(self, at, buf, send, recv, start=0, size=None):
        self.at, self.buf, self.send, self.recv = at, buf, send, recv
        self.base, self.size = start, buf.shape[1] if size is None else size
        self.half = self.size // 2
        self.sent = []

    def view(self, piece, half=None):
        if half is None:
            return self.buf.at[piece, pl.ds(self.base, self.size)]
        return self.buf.at[piece, pl.ds(self.base + half * self.half, self.half)]

    def copy(self, index, piece, device, half=None):
        ref = self.view(piece, half)
        return pltpu.make_async_remote_copy(
            src_ref=ref,
            dst_ref=ref,
            send_sem=self.send.at[index],
            recv_sem=self.recv.at[index],
            device_id=device,
            device_id_type=MESH,
        )

    def go(self, index, piece, device, half=None):
        descriptor = self.copy(index, piece, device, half)
        descriptor.start()
        self.sent.append(descriptor)

    def arrived(self, index, piece, half=None):
        self.copy(index, piece, self.at.sibling(), half).wait_recv()

    def to_sibling(self, qa, qb):
        index = 20 + 4 * RING.index(qa) + RING.index(qb)
        self.go(index, self.at.piece(qa, qb), self.at.sibling())

    def spread(self, qa):
        index = 4 + 4 * RING.index(qa)
        piece = self.at.piece(qa, 0)
        self.go(index, piece, self.at.device(0, 1))
        self.go(index + 1, piece, self.at.device(0, -1))
        self.to_sibling(qa, 0)

    def start(self):
        piece = self.at.piece(0, 0)
        self.go(0, piece, self.at.device(1, 0))
        self.go(1, piece, self.at.device(-1, 0))
        self.spread(0)

    def first_axis(self):
        low, high = self.at.piece(-1, 0), self.at.piece(1, 0)
        self.arrived(0, low)
        self.go(2, low, self.at.device(1, 0), 0)
        self.arrived(1, high)
        self.go(3, high, self.at.device(-1, 0), 1)
        self.spread(-1)
        self.spread(1)

    def first_axis_far(self):
        far = self.at.piece(2, 0)
        self.arrived(2, far, 0)
        self.arrived(3, far, 1)
        self.spread(2)

    def relay(self, qa):
        index = 4 + 4 * RING.index(qa)
        low, high = self.at.piece(qa, -1), self.at.piece(qa, 1)
        self.arrived(index, low)
        self.go(index + 2, low, self.at.device(0, 1), 0)
        self.arrived(index + 1, high)
        self.go(index + 3, high, self.at.device(0, -1), 1)
        self.to_sibling(qa, -1)
        self.to_sibling(qa, 1)

    def far(self, qa):
        index = 4 + 4 * RING.index(qa)
        piece = self.at.piece(qa, 2)
        self.arrived(index + 2, piece, 0)
        self.arrived(index + 3, piece, 1)
        self.to_sibling(qa, 2)

    def from_sibling(self, qa):
        for qb in RING:
            index = 20 + 4 * RING.index(qa) + RING.index(qb)
            self.arrived(index, self.at.piece(qa, qb, 1 - self.at.core))

    def own_group(self, qa):
        return [self.at.piece(qa, qb) for qb in RING]

    def sibling_group(self, qa):
        return [self.at.piece(qa, qb, 1 - self.at.core) for qb in RING]

    def steps(self):
        return [
            self.start,
            self.first_axis,
            self.first_axis_far,
            functools.partial(self.relay, 0),
            functools.partial(self.relay, -1),
            functools.partial(self.relay, 1),
            functools.partial(self.relay, 2),
            functools.partial(self.far, 0),
            functools.partial(self.far, -1),
            functools.partial(self.far, 1),
            functools.partial(self.far, 2),
        ]

    def finish(self):
        for descriptor in self.sent:
            descriptor.wait_send()


POSITION = {0: 0, 1: 1, 7: 2, 2: 3, 6: 4, 3: 5, 5: 6, 4: 7}
NEAR = 5
SIZE = (NEAR * 160, (8 - NEAR) * 160)
WHOLE = SIZE[0] // 256 * 256
LEFT = SIZE[0] - WHOLE
PARTS = 4
CAP = 40


def kernel(
    attn_hbm, context_ref, residual_ref, cot_ref, ids_ref, gates_ref, gain1_ref, wg_ref, wu_ref, wd_ref,
    og_ref, ou_ref, od_ref,
    rows_in0, rows_in1, rows_cot0, rows_cot1, ctx_all, wgu, wd, wtmp, acc0, acc1, back0, back1, ssq0, ssq1, dgu0, dgu1, hid0, hid1,
    part_gu, part_d, stage, gain_ref, attn_ref,
    red_in_l, red_in_s, red_out_l, red_out_s, red_sum, merged_all, attn_acc,
    res_all, cot_all, info_all, sel, route_x, route_c,
    w_sem, in0_send, in0_recv, in1_send, in1_recv,
    cotz_send, cotz_recv, cot0_send, cot0_recv, cot1_send, cot1_recv,
    ctx_send, ctx_recv, in_local, ex_send, ex_recv, ex_local,
    rl_send, rl_recv, rs_send, rs_recv, ma_send, ma_recv, ga_send, ga_recv,
    tx_send, tx_recv, tc_send, tc_recv, out_sem,
):
    at = Coords()
    z, mp, dp = at.z, at.mp, at.dp
    own = at.piece(0, 0)
    hidden = wg_ref.shape[0]
    hid_pad = wgu.shape[0] // 2
    rows_in = (rows_in0, rows_in1)
    acc, acc_back, ssq, dgu, hid = (acc0, acc1), (back0, back1), (ssq0, ssq1), (dgu0, dgu1), (hid0, hid1)
    rows_cot = (rows_cot0, rows_cot1)
    pending = []

    def z_dev(k):
        return (lax.rem(z + k + 8, 8), mp, dp)

    def mp_dev(k):
        return (z, lax.rem(mp + k, 8), dp)

    def dp_dev(k):
        return (z, mp, lax.rem(dp + k, 4))

    def remote(src, dst, send, recv, device):
        return pltpu.make_async_remote_copy(
            src_ref=src, dst_ref=dst, send_sem=send, recv_sem=recv,
            device_id=device, device_id_type=MESH,
        )

    def push(src, dst, send, recv, device):
        descriptor = remote(src, dst, send, recv, device)
        descriptor.start()
        pending.append(descriptor)

    def landed(dst, recv, send):
        remote(dst, dst, send, recv, at.sibling()).wait_recv()

    barrier = pltpu.get_barrier_semaphore()
    peers = [z_dev(k) for k in range(1, 8)] + [mp_dev(k) for k in range(1, 8)]
    peers += [dp_dev(k) for k in range(1, 4)]
    for dy in (1, -1):
        y = lax.rem(at.y + dy + 4, 4)
        peers.append((z, lax.rem(y, 2) * 4 + at.x, lax.div(y, 2) * 2 + at.core))
    for peer in peers:
        pl.semaphore_signal(barrier, inc=1, device_id=peer, device_id_type=MESH)

    ctx_copy = pltpu.make_async_copy(context_ref, ctx_all.at[own], in_local.at[0])
    ctx_copy.start()
    dp_rows = pl.ds(pl.multiple_of(dp * 128, 128), 128)

    def columns(k):
        d = lax.rem(dp + k, 4)
        return pl.ds(pl.multiple_of(d * 1024 + mp * 128, 128), 128)

    locals_ = [
        pltpu.make_async_copy(residual_ref.at[:, columns(0)], res_all.at[dp_rows], ex_local.at[0]),
        pltpu.make_async_copy(cot_ref.at[:, columns(0)], cot_all.at[dp_rows], ex_local.at[1]),
    ]
    attn_copy = pltpu.make_async_copy(attn_hbm, attn_ref, in_local.at[1])
    attn_copy.start()
    for copy in locals_:
        copy.start()

    gain_ref[...] = gain1_ref[...].astype(F32).reshape(32, 128)

    ids = ids_ref[...]
    experts = lax.broadcasted_iota(jnp.int32, (8, 128), 0)
    first = jnp.where(experts == ids[0:1, :], 1.0, 0.0)
    second = jnp.where(experts == ids[1:2, :], 1.0, 0.0)
    before = jnp.where(
        lax.broadcasted_iota(jnp.int32, (128, 128), 0) < lax.broadcasted_iota(jnp.int32, (128, 128), 1),
        1.0, 0.0,
    ).astype(BF)
    counts = jnp.dot(
        jnp.concatenate([first, second], axis=0).astype(BF), before, preferred_element_type=F32
    )
    slot0 = jnp.sum(first * counts[0:8], axis=0, keepdims=True)
    slot1 = jnp.sum(
        second * (counts[8:16] + jnp.sum(first, axis=1, keepdims=True)), axis=0, keepdims=True
    )
    base = (ids * 160 + dp * CAP).astype(F32)
    code0 = jnp.where(slot0 < CAP, base[0:1] + slot0, -1.0)
    code1 = jnp.where(slot1 < CAP, base[1:2] + slot1, -1.0)
    gates = gates_ref[...].astype(F32) / 32768.0
    info_all[dp] = jnp.concatenate([code0, code1, gates, jnp.zeros((4, 128), F32)], axis=0)
    pl.semaphore_wait(barrier, len(peers))

    for k in range(1, 4):
        push(cot_ref.at[:, columns(k)], cot_all.at[dp_rows], ex_send.at[0, k], ex_recv.at[0, k], dp_dev(k))
        push(info_all.at[dp], info_all.at[dp], ex_send.at[1, k], ex_recv.at[1, k], dp_dev(k))

    def chunk(k):
        t = lax.rem(z + k + 8, 8)
        return pl.ds(pl.multiple_of(t * 64, 64), 64)

    width = 1024 // PARTS
    part_cols = [pl.ds(h * width, width) for h in range(PARTS)]

    def reduce_step(step):
        for h in range(PARTS):
            cols = part_cols[h]
            sign = 1 - 2 * (h % 2)
            if step < 4:
                part = chunk(sign * (4 - step))
                src = attn_hbm.at[part, cols]
                if step > 0:
                    landed(red_in_l.at[step - 1, h], rl_recv.at[step - 1, h], rl_send.at[step - 1, h])
                    red_out_l[step - 1, h] = (
                        red_in_l[step - 1, h].astype(F32) + attn_ref[part, cols].astype(F32)
                    ).astype(BF)
                    src = red_out_l.at[step - 1, h]
                push(src, red_in_l.at[step, h], rl_send.at[step, h], rl_recv.at[step, h], z_dev(sign))
            if step < 3:
                part = chunk(-sign * (3 - step))
                src = attn_hbm.at[part, cols]
                if step > 0:
                    landed(red_in_s.at[step - 1, h], rs_recv.at[step - 1, h], rs_send.at[step - 1, h])
                    red_out_s[step - 1, h] = (
                        red_in_s[step - 1, h].astype(F32) + attn_ref[part, cols].astype(F32)
                    ).astype(BF)
                    src = red_out_s.at[step - 1, h]
                push(src, red_in_s.at[step, h], rs_send.at[step, h], rs_recv.at[step, h], z_dev(-sign))

    reduce_step(0)

    ctx_gather = PlaneGather(at, ctx_all, ctx_send, ctx_recv)
    rest = SIZE[0] - 160
    cot_gather = (
        PlaneGather(at, rows_cot0, cot0_send, cot0_recv, 160, rest),
        PlaneGather(at, rows_cot1, cot1_send, cot1_recv),
        PlaneGather(at, rows_cot0, cotz_send, cotz_recv, 0, 160),
    )
    in_gather = (
        PlaneGather(at, rows_in0, in0_send, in0_recv),
        PlaneGather(at, rows_in1, in1_send, in1_recv),
    )
    ctx_steps = ctx_gather.steps()
    cot_steps = [gather.steps() for gather in cot_gather]
    in_steps = [gather.steps() for gather in in_gather]

    def run(steps, count=1):
        for _ in range(count):
            if steps:
                steps.pop(0)()

    ctx_copy.wait()
    run(ctx_steps)

    weights = [
        pltpu.make_async_copy(wg_ref, wtmp.at[0], w_sem.at[0]),
        pltpu.make_async_copy(wu_ref, wtmp.at[1], w_sem.at[1]),
        pltpu.make_async_copy(wd_ref, wd, w_sem.at[2]),
    ]
    for copy in weights:
        copy.start()

    def from_group(k):
        d = lax.rem(dp - k + 4, 4)
        return pl.ds(pl.multiple_of(d * 128, 128), 128), d

    attn_copy.wait()
    reduce_step(1)
    locals_[1].wait()
    for k in range(1, 4):
        rows, d = from_group(k)
        landed(cot_all.at[rows], ex_recv.at[0, k], ex_send.at[0, k])
        landed(info_all.at[d], ex_recv.at[1, k], ex_send.at[1, k])

    @pl.loop(0, 8, unroll=2)
    def _(e):
        place = (lax.broadcasted_iota(jnp.int32, (160, 128), 0) + e * 160).astype(F32)
        row_gate = jnp.zeros((160, 1), F32)
        rows = pl.ds(pl.multiple_of(e * 160, 160), 160)
        for d in range(4):
            info = info_all[d]
            first = place == info[0:1, :]
            second = place == info[1:2, :]
            sel[rows, d * 128:(d + 1) * 128] = jnp.where(first | second, 1.0, 0.0).astype(BF)
            gates = jnp.where(first, info[2:3, :], jnp.where(second, info[3:4, :], 0.0))
            row_gate += jnp.sum(gates, axis=1, keepdims=True)
        picked = jnp.dot(sel[rows, :], cot_all[...], preferred_element_type=F32)
        route_c[e] = (picked * row_gate).astype(BF)

    def block(k):
        place = POSITION[k]
        if place < NEAR:
            return 0, pl.ds(place * 160, 160)
        return 1, pl.ds((place - NEAR) * 160, 160)

    def exchange(route, gathered, send, recv, wanted):
        if wanted == 0:
            half, rows = block(0)
            gathered[half][own, rows, :] = route[z]
        for k in sorted(range(1, 8), key=lambda k: POSITION[k]):
            half, rows = block(k)
            e = lax.rem(z - k + 8, 8)
            if half == wanted:
                push(route.at[e], gathered[half].at[own, rows], send.at[k], recv.at[k], z_dev(-k))

    def exchanged(gathered, send, recv, wanted):
        for k in range(1, 8):
            half, rows = block(k)
            if half == wanted:
                landed(gathered[half].at[own, rows], recv.at[k], send.at[k])

    cot_near, cot_far, cot_own = cot_steps
    in_near, in_far = in_steps
    run(ctx_steps)
    reduce_step(2)
    exchange(route_c, rows_cot, tc_send, tc_recv, 0)
    run(cot_own)
    for k in range(1, 4):
        push(residual_ref.at[:, columns(k)], res_all.at[dp_rows], ex_send.at[2, k], ex_recv.at[2, k], dp_dev(k))
    run(ctx_steps, 2)
    reduce_step(3)
    run(cot_own)
    run(ctx_steps, 2)

    for h in range(PARTS):
        landed(red_in_l.at[3, h], rl_recv.at[3, h], rl_send.at[3, h])
        landed(red_in_s.at[2, h], rs_recv.at[2, h], rs_send.at[2, h])
        total = (
            red_in_l[3, h].astype(F32) + red_in_s[2, h].astype(F32)
            + attn_ref[chunk(0), part_cols[h]].astype(F32)
        )
        mean = (total * 0.125).astype(BF)
        for part in range(8 // PARTS):
            red_sum[8 // PARTS * h + part] = mean[:, part * 128:(part + 1) * 128]
    own_rows = pl.ds(pl.multiple_of(z * 64, 64), 64)
    for k in range(1, 8):
        j = lax.rem(mp + k, 8)
        push(red_sum.at[j], merged_all.at[mp, own_rows], ma_send.at[k], ma_recv.at[k], mp_dev(k))
    merged_all[mp, own_rows, :] = red_sum[mp]
    exchange(route_c, rows_cot, tc_send, tc_recv, 1)
    exchanged(rows_cot, tc_send, tc_recv, 0)
    run(cot_near)
    run(ctx_steps)
    run(cot_own, 2)
    for k in range(1, 8):
        j = lax.rem(mp - k + 8, 8)
        landed(merged_all.at[j, own_rows], ma_recv.at[k], ma_send.at[k])

    def merged_view(k, h):
        t = lax.rem(z + k + 8, 8)
        return merged_all.at[pl.ds(8 // PARTS * h, 8 // PARTS), pl.ds(pl.multiple_of(t * 64, 64), 64)]

    def gather_step(step):
        for h in range(PARTS):
            sign = 1 - 2 * (h % 2)
            if step > 0:
                landed(merged_view(-sign * step, h), ga_recv.at[0, step - 1, h], ga_send.at[0, step - 1, h])
            if step < 4:
                view = merged_view(-sign * step, h)
                push(view, view, ga_send.at[0, step, h], ga_recv.at[0, step, h], z_dev(sign))
            if 0 < step < 4:
                landed(merged_view(sign * step, h), ga_recv.at[1, step - 1, h], ga_send.at[1, step - 1, h])
            if step < 3:
                view = merged_view(sign * step, h)
                push(view, view, ga_send.at[1, step, h], ga_recv.at[1, step, h], z_dev(-sign))

    gather_step(0)
    run(ctx_steps, 2)
    run(cot_own, 2)
    run(cot_near)
    gather_step(1)
    run(cot_near, 2)
    exchanged(rows_cot, tc_send, tc_recv, 1)
    run(cot_far)
    run(ctx_steps, 2)
    gather_step(2)
    run(cot_near, 2)
    run(cot_own)
    gather_step(3)
    run(cot_far)
    run(cot_near)
    for qa in RING:
        ctx_gather.from_sibling(qa)
    for k in range(1, 4):
        rows, _ = from_group(k)
        landed(res_all.at[rows], ex_recv.at[2, k], ex_send.at[2, k])
    locals_[0].wait()

    last = lax.div(lax.rem(z + 4, 8), 2)

    def feature_product(terms):
        context = jnp.concatenate(
            [
                jnp.concatenate([ctx_all[d * 8 + j, :, pairs] for j, pairs in terms], axis=1)
                for d in range(4)
            ],
            axis=0,
        )
        weight = jnp.concatenate([merged_all[j, pairs, :] for j, pairs in terms], axis=0)
        return jnp.dot(context, weight, preferred_element_type=F32)

    def pair_of(k):
        return pl.ds(pl.multiple_of(lax.rem(last + k, 4) * 128, 128), 128)

    attn_acc[...] = res_all[...].astype(F32)
    for j in range(0, 8, 2):
        attn_acc[...] += feature_product([(j + i, pair_of(k)) for i in range(2) for k in range(1, 4)])
    gather_step(4)

    def lanes(piece):
        return pl.ds(pl.multiple_of(piece * 128, 128), 128)

    def gain_of(piece):
        return gain_ref[pl.ds(piece, 1), :]

    attn_acc[...] += feature_product([(j, pair_of(0)) for j in range(8)])
    res_all[...] = (attn_acc[...] * gain_of(own)).astype(BF)

    picked = jnp.dot(sel[...], res_all[...], preferred_element_type=F32).astype(BF)
    route_x[...] = picked.reshape(8, 160, 128)

    exchange(route_x, rows_in, tx_send, tx_recv, 0)

    for copy in weights:
        copy.wait()
    wgu[0:hidden, :] = wtmp[0]
    wgu[hid_pad:hid_pad + hidden, :] = wtmp[1]
    for ref in acc + acc_back + ssq:
        ref[...] = jnp.zeros_like(ref)

    def tiles(half):
        return [(start, min(256, SIZE[half] - start)) for start in range(0, SIZE[half], 256)]

    def back_group(half, group):
        lhs = jnp.concatenate([wd[:, lanes(p)] for p in group], axis=1)
        for start, width in tiles(half):
            rhs = jnp.concatenate([rows_cot[half][p, start:start + width, :] for p in group], axis=1)
            cols = slice(start, start + width)
            acc_back[half][:, cols] += lax.dot_general(lhs, rhs, NT, preferred_element_type=F32)

    def fore_group(half, group):
        lhs = jnp.concatenate([wgu[:, lanes(p)] for p in group], axis=1)
        inverse = [1.0 / gain_of(p) for p in group]
        for start, width in tiles(half):
            parts = [rows_in[half][p, start:start + width, :] for p in group]
            cols = slice(start, start + width)
            acc[half][:, cols] += lax.dot_general(
                lhs, jnp.concatenate(parts, axis=1), NT, preferred_element_type=F32
            )
            squares = ssq[half][cols, :]
            for part, scale in zip(parts, inverse):
                value = part.astype(F32) * scale
                squares += value * value
            ssq[half][cols, :] = squares

    def own_back(half, *places):
        for qa in places:
            back_group(half, cot_gather[half].own_group(qa))

    def sibling_back(half, *places):
        for qa in places:
            if half == 0:
                cot_gather[2].from_sibling(qa)
            cot_gather[half].from_sibling(qa)
            back_group(half, cot_gather[half].sibling_group(qa))

    def own_fore(half, *places):
        for qa in places:
            fore_group(half, in_gather[half].own_group(qa))

    def sibling_fore(half, *places):
        for qa in places:
            in_gather[half].from_sibling(qa)
            fore_group(half, in_gather[half].sibling_group(qa))

    def activations(half):
        for start in range(0, SIZE[half], 128):
            cols = slice(start, min(start + 128, SIZE[half]))
            into, place = half, cols
            if half == 0 and start >= WHOLE:
                into, place = 1, slice(SIZE[1] + start - WHOLE, SIZE[1] + cols.stop - WHOLE)
            squares = lax.dot_general(
                jnp.ones((8, 128), BF), ssq[half][cols, :].astype(BF), NT, preferred_element_type=F32
            )
            inv = lax.rsqrt(squares[0:1] * (1.0 / 4096.0) + 1e-05)
            gate = acc[half][0:hidden, cols] * inv
            up = acc[half][hid_pad:hid_pad + hidden, cols] * inv
            back = acc_back[half][:, cols]
            sig = jax.nn.sigmoid(gate)
            active = gate * sig
            hid[into][:, place] = (active * up).astype(BF)
            back = back * inv
            dgu[into][0:hidden, place] = (back * up * sig * (1.0 + gate * (1.0 - sig))).astype(BF)
            dgu[into][hid_pad:hid_pad + hidden, place] = (back * active).astype(BF)

    def contracted(half, parts, n):
        if half == 0:
            pair = [parts[0][2 * n + i, 0:WHOLE, :] for i in range(2)]
        else:
            pair = [
                jnp.concatenate([parts[1][2 * n + i], parts[0][2 * n + i, WHOLE:WHOLE + LEFT, :]], axis=0)
                for i in range(2)
            ]
        return jnp.concatenate(pair, axis=1)

    def gradients(half, chunk):
        @pl.loop(0, 4, unroll=4)
        def _(i):
            n = chunk * 4 + i
            cols = pl.ds(pl.multiple_of(n * 256, 256), 256)
            both = jnp.dot(dgu[half][...], contracted(half, rows_in, n), preferred_element_type=F32)
            down = jnp.dot(hid[half][...], contracted(half, rows_cot, n), preferred_element_type=F32)
            if half == 0:
                part_gu[:, cols] = both
                part_d[:, cols] = down
            else:
                both = (both + part_gu[:, cols]).astype(BF)
                stage[0, :, cols] = both[0:hidden]
                stage[1, :, cols] = both[hid_pad:hid_pad + hidden]
                stage[2, :, cols] = (down + part_d[:, cols]).astype(BF)

    run(cot_far, 3)
    run(cot_near, 2)
    run(cot_far)
    run(cot_near, 2)
    exchanged(rows_in, tx_send, tx_recv, 0)
    run(in_near)
    run(cot_far)
    run(cot_own, 4)
    run(cot_far, 3)
    own_back(0, 0, -1, 1, 2)
    run(in_near)
    run(cot_far)
    exchange(route_x, rows_in, tx_send, tx_recv, 1)
    sibling_back(0, 0, -1)
    run(in_near)
    sibling_back(0, 1, 2)
    run(in_near, 3)
    exchanged(rows_in, tx_send, tx_recv, 1)
    run(in_far)
    own_back(1, 0, -1, 1, 2)
    run(in_near)
    sibling_back(1, 0, -1, 1, 2)
    run(in_near)
    own_fore(0, 0)
    run(in_near)
    own_fore(0, -1)
    run(in_far)
    run(in_near)
    own_fore(0, 1)
    run(in_near)
    run(in_far)
    own_fore(0, 2)
    run(in_far)
    sibling_fore(0, 0)
    run(in_far)
    sibling_fore(0, -1)
    run(in_far)
    sibling_fore(0, 1)
    sibling_fore(0, 2)
    activations(0)
    run(in_far)
    gradients(0, 0)
    run(in_far, 2)
    gradients(0, 1)
    run(in_far, 2)
    gradients(0, 2)
    gradients(0, 3)
    own_fore(1, 0, -1, 1, 2)
    sibling_fore(1, 0, -1, 1, 2)
    activations(1)
    outs = (og_ref, ou_ref, od_ref)
    writes = []
    for quarter in range(4):
        gradients(1, quarter)
        cols = pl.ds(quarter * 1024, 1024)
        for index in range(3):
            write = pltpu.make_async_copy(
                stage.at[index, :, cols], outs[index].at[:, cols], out_sem.at[index, quarter]
            )
            write.start()
            writes.append(write)

    assert not any([ctx_steps] + cot_steps + in_steps)
    for gather in (ctx_gather,) + cot_gather + in_gather:
        gather.finish()
    for descriptor in pending:
        descriptor.wait_send()
    for write in writes:
        write.wait()


def write_kernel(*refs):
    count = 3
    sources, outs, hold, sem_in, sem_out = refs[:count], refs[count:2 * count], *refs[2 * count:]
    reads, writes = [], []
    for index in range(count):
        for part in range(4):
            cols = pl.ds(part * 1024, 1024)
            there = hold.at[index, :, cols]
            reads.append(pltpu.make_async_copy(sources[index].at[:, cols], there, sem_in.at[index, part]))
            writes.append(pltpu.make_async_copy(there, outs[index].at[:, cols], sem_out.at[index, part]))
    for read in reads:
        read.start()
    for read, write in zip(reads, writes):
        read.wait()
        write.start()
    for write in writes:
        write.wait()


def per_device(
    context, residual, attn_weight, norm_gain, gate_weight, up_weight, down_weight,
    cotangent, expert_ids, gate_fixed,
):
    hidden = gate_weight.shape[2]
    pad = 176
    dma = pltpu.SemaphoreType.DMA
    vmem = pl.BlockSpec(memory_space=pltpu.VMEM)
    hbm = pl.BlockSpec(memory_space=pl.ANY)
    out = jax.ShapeDtypeStruct((hidden, 4096), BF)
    copies = PlaneGather.COPIES
    near, far = SIZE
    grads = pl.pallas_call(
        kernel,
        out_shape=(out, out, out),
        in_specs=[hbm, hbm, hbm, hbm, vmem, vmem, vmem, hbm, hbm, hbm],
        out_specs=(hbm, hbm, hbm),
        scratch_shapes=[
            pltpu.VMEM((32, near, 128), BF),
            pltpu.VMEM((32, far, 128), BF),
            pltpu.VMEM((32, near, 128), BF),
            pltpu.VMEM((32, far, 128), BF),
            pltpu.VMEM((32, 128, 512), BF),
            pltpu.VMEM((2 * pad, 4096), BF),
            pltpu.VMEM((hidden, 4096), BF),
            pltpu.VMEM((2, hidden, 4096), BF),
            pltpu.VMEM((2 * pad, near), F32),
            pltpu.VMEM((2 * pad, far), F32),
            pltpu.VMEM((hidden, near), F32),
            pltpu.VMEM((hidden, far), F32),
            pltpu.VMEM((near, 128), F32),
            pltpu.VMEM((far, 128), F32),
            pltpu.VMEM((2 * pad, WHOLE), BF),
            pltpu.VMEM((2 * pad, far + LEFT), BF),
            pltpu.VMEM((hidden, WHOLE), BF),
            pltpu.VMEM((hidden, far + LEFT), BF),
            pltpu.VMEM((2 * pad, 4096), F32),
            pltpu.VMEM((hidden, 4096), F32),
            pltpu.VMEM((3, hidden, 4096), BF),
            pltpu.VMEM((32, 128), F32),
            pltpu.VMEM((512, 1024), BF),
            pltpu.VMEM((4, PARTS, 64, 1024 // PARTS), BF),
            pltpu.VMEM((3, PARTS, 64, 1024 // PARTS), BF),
            pltpu.VMEM((3, PARTS, 64, 1024 // PARTS), BF),
            pltpu.VMEM((2, PARTS, 64, 1024 // PARTS), BF),
            pltpu.VMEM((8, 64, 128), BF),
            pltpu.VMEM((8, 512, 128), BF),
            pltpu.VMEM((512, 128), F32),
            pltpu.VMEM((512, 128), BF),
            pltpu.VMEM((512, 128), BF),
            pltpu.VMEM((4, 8, 128), F32),
            pltpu.VMEM((1280, 512), BF),
            pltpu.VMEM((8, 160, 128), BF),
            pltpu.VMEM((8, 160, 128), BF),
            dma((3,)),
            dma((copies,)), dma((copies,)), dma((copies,)), dma((copies,)),
            dma((copies,)), dma((copies,)), dma((copies,)), dma((copies,)),
            dma((copies,)), dma((copies,)),
            dma((copies,)), dma((copies,)), dma((2,)),
            dma((3, 4)), dma((3, 4)), dma((2,)),
            dma((4, PARTS)), dma((4, PARTS)), dma((3, PARTS)), dma((3, PARTS)),
            dma((8,)), dma((8,)),
            dma((2, 4, PARTS)), dma((2, 4, PARTS)),
            dma((8,)), dma((8,)),
            dma((8,)), dma((8,)),
            dma((3, 4)),
        ],
        compiler_params=pltpu.CompilerParams(
            collective_id=0, has_side_effects=True, vmem_limit_bytes=67_000_000
        ),
    )(
        attn_weight[0], context, residual, cotangent, expert_ids.T, gate_fixed.T, norm_gain,
        gate_weight[0].T, up_weight[0].T, down_weight[0],
    )
    grads = pl.pallas_call(
        write_kernel,
        out_shape=(out, out, out),
        in_specs=[hbm, hbm, hbm],
        out_specs=(hbm, hbm, hbm),
        scratch_shapes=[pltpu.VMEM((3, hidden, 4096), BF), dma((3, 4)), dma((3, 4))],
    )(*grads)
    return grads[0].T[None], grads[1].T[None], grads[2][None]


def solution(mesh):
    return jax.shard_map(
        per_device,
        mesh=mesh,
        in_specs=(
            P(("branch", "dp"), "mp"),
            P(("branch", "dp"), None),
            P("branch", "mp", "dp"),
            P(),
            P("branch", None, ("mp", "dp")),
            P("branch", None, ("mp", "dp")),
            P("branch", ("mp", "dp"), None),
            P(("branch", "dp"), None),
            P(("branch", "dp"), None),
            P(("branch", "dp"), None),
        ),
        out_specs=(
            P("branch", None, ("mp", "dp")),
            P("branch", None, ("mp", "dp")),
            P("branch", ("mp", "dp"), None),
        ),
        check_vma=False,
    )
```
